256 devices in a mesh: event: 4 (over z_lo, core), space: 64 (over x, z_hi, y).
Axes of the slice: x: 4, y: 4, z: 8 (z_hi: 4, z_lo: 2; z = z_hi * 2 + z_lo), core: 2. Of those that a mesh axis runs over, the one named last changes fastest.
Arguments:
- state_now: float32 [4, 512, 16, 512], P('event', 'space'), may hold values from -6 to 6
- state_prev: float32 [4, 512, 16, 512], P('event', 'space'), may hold values from -6 to 6
- adjoint_now: float32 [4, 512, 16, 512], P('event', 'space'), may hold values from -1.8 to 1.8
- adjoint_next: float32 [4, 512, 16, 512], P('event', 'space'), may hold values from -1.8 to 1.8
- modulus: float32 [5, 128, 5, 4, 5, 128], P(None, 'space'), may hold values from 0.5 to 2
- density: float32 [512, 16, 512], P('space'), may hold values from 0.5 to 2
- receivers: int32 [8192], P('space'), may hold values from 0 to 65535
- observed: float32 [4, 3, 8192], P('event', None, 'space'), may hold values from -12 to 12
Outputs:
- kernel: float32 [5, 128, 5, 4, 5, 128], P(None, 'space', None, 'event')
- misfit: float32 [4], P('event')
The draws below stay inside these ranges and needn't reach their ends.
Inputs may be any that keep to these rules, and one draw needn't show every extreme that they name: A node of the receiver's own slab, numbered with the third index fastest over 8 x 16 x 512 nodes; two receivers may share a node.
All inputs are finite; a program needn't handle non-finite values. Where the reference program divides by a largest or mean magnitude, that divisor is 1e-20 or more.
Results may differ from the reference program's by a relative error of at most 0.00011.
Values sent between devices are 32-bit elements; how exact they have to be, the bound alone decides.
No kernel may reach another device: no remote copies, remote signals or barrier semaphores. Data moves between devices by JAX's collectives and lax.ppermute only.
A program may use at most 64 MiB of HBM per device.

```python
import math
import jax
import jax.numpy as jnp
import numpy as np
from jax import lax

NODES_1D = 5
EXD = 2
EY = 4
EZ = 128
REC_DEV = 128
NT = 3
EX = 128
EVENTS = 4
RECEIVERS = 8192
NX = 512
NY = 16
NZ = 512
NODES_DEV = 65536


def draw_observed(key, part):
    position = jnp.arange(RECEIVERS, dtype=jnp.float32)
    rising = 1.0 + 2.0 * position / (RECEIVERS - 1)
    values = jax.random.truncated_normal(key, -4.0, 4.0, (EVENTS, NT, RECEIVERS), jnp.float32)
    return values * rising


def plant(entries, key, least, top_value):
    dims = entries.shape
    index_at = [jax.random.randint(jax.random.fold_in(key, axis), (), 0, dims[axis]) for axis in range(len(dims))]
    entries = entries.at[tuple(index_at)].set(least)
    longest = dims.index(max(dims))
    index_at[longest] = (index_at[longest] + 1) % dims[longest]
    return entries.at[tuple(index_at)].set(top_value)


def steps_of(stream_key, shape, shards, least, top_value):
    level = 1.0
    for dim, blocks in shards:
        steps = jax.random.uniform(jax.random.fold_in(jax.random.fold_in(stream_key, 6), dim), (blocks,), jnp.float32, least / len(shards), top_value / len(shards))
        level = level * jnp.repeat(jnp.exp(steps), shape[dim] // blocks).reshape((-1,) + (1,) * (len(shape) - 1 - dim))
    return level


def scatter_about(rng, extent, deviation, bound, split=(), kind=jnp.bfloat16):
    gain = steps_of(rng, extent, split, -0.22, 0.18) if split else 1.0
    entries = jax.random.normal(rng, extent, jnp.float32) * deviation * gain
    return jnp.minimum(jnp.maximum(entries, -bound), bound).astype(kind)


def setup_inputs(seed: int = 0) -> dict:
    key_list = jax.random.split(jax.random.key(seed), 9)
    state_now = scatter_about(key_list[0], (EVENTS, NX, NY, NZ), 1.0, 6.0, ((0, 4), (1, 64)), jnp.float32)
    state_prev = scatter_about(key_list[1], (EVENTS, NX, NY, NZ), 1.0, 6.0, ((0, 4), (1, 64)), jnp.float32)
    adjoint_now = scatter_about(key_list[2], (EVENTS, NX, NY, NZ), 0.3, 1.8, ((0, 4), (1, 64)), jnp.float32)
    adjoint_next = scatter_about(key_list[3], (EVENTS, NX, NY, NZ), 0.3, 1.8, ((0, 4), (1, 64)), jnp.float32)
    modulus = jnp.clip(jnp.exp(math.log(2.0) - 1.3862944 * jax.random.uniform(key_list[4], (NODES_1D, EX, NODES_1D, EY, NODES_1D, EZ), jnp.float32) ** steps_of(key_list[4], (NODES_1D, EX, NODES_1D, EY, NODES_1D, EZ), ((1, 64),), -0.2, 0.2)), 0.5, 2.0)
    density = jnp.clip(jnp.exp(math.log(2.0) - 1.3862944 * jax.random.uniform(key_list[5], (NX, NY, NZ), jnp.float32) ** steps_of(key_list[5], (NX, NY, NZ), ((0, 64),), -0.2, 0.2)), 0.5, 2.0)
    receivers = plant(jax.random.randint(key_list[6], (RECEIVERS,), 0, NODES_DEV), jax.random.fold_in(key_list[6], 1), 0, NODES_DEV - 1).astype(jnp.int32)
    observed = draw_observed(jax.random.fold_in(key_list[8], 71), 0)
    return {"state_now": state_now, "state_prev": state_prev, "adjoint_now": adjoint_now, "adjoint_next": adjoint_next, "modulus": modulus, "density": density, "receivers": receivers, "observed": observed}


TIME_STEP = 0.05
EPSILON = 1e-06

def gll_tables():
    root = math.sqrt(3.0 / 7.0)
    points = np.array([-1.0, -root, 0.0, root, 1.0])
    weights = np.array([0.1, 49.0 / 90.0, 32.0 / 45.0, 49.0 / 90.0, 0.1])
    legendre = (35.0 * points ** 4 - 30.0 * points ** 2 + 3.0) / 8.0
    derivative = np.zeros((5, 5))
    for row in range(5):
        for column in range(5):
            if row != column:
                derivative[row, column] = legendre[row] / (legendre[column] * (points[row] - points[column]))
    derivative[0, 0] = -5.0
    derivative[4, 4] = 5.0
    return (jnp.asarray(derivative, dtype=jnp.float32), jnp.asarray(weights, dtype=jnp.float32))

def cube_of(weights):
    return weights[:, None, None, None, None, None] * weights[None, None, :, None, None, None] * weights[None, None, None, None, :, None]

def line_weights(length, first_index):
    indices = first_index + jnp.arange(length, dtype=jnp.int32)
    position = indices % 4
    values = jnp.where(position == 1, 49.0 / 90.0, jnp.where(position == 2, 32.0 / 45.0, jnp.where(position == 3, 49.0 / 90.0, 0.2)))
    return jnp.where(indices == 0, 0.1, values).astype(jnp.float32)

def split_axis(field, axis_at, elements):
    pieces = [lax.slice_in_dim(field, offset, offset + 4 * (elements - 1) + 1, stride=4, axis=axis_at) for offset in range(5)]
    return jnp.stack(pieces, axis=axis_at)

def merge_axis(blocks, axis_at, elements):
    pieces = [lax.index_in_dim(blocks, offset, axis_at, keepdims=False) for offset in range(5)]
    zero_part = jnp.zeros_like(pieces[4])
    new_shape = pieces[0].shape[:axis_at] + (4 * elements,) + pieces[0].shape[axis_at + 1:]
    leading = jnp.stack(pieces[:4], axis=axis_at + 1).reshape(new_shape)
    trailing = jnp.stack([pieces[4], zero_part, zero_part, zero_part], axis=axis_at + 1).reshape(new_shape)
    pad_lead = [(0, 0)] * len(new_shape)
    pad_rear = [(0, 0)] * len(new_shape)
    pad_lead[axis_at] = (0, 1)
    pad_rear[axis_at] = (4, 0)
    leading = jnp.pad(leading, pad_lead)
    trailing = lax.slice_in_dim(jnp.pad(trailing, pad_rear), 0, 4 * elements + 1, axis=axis_at)
    return leading + trailing

def to_elements(nodes, count_x, count_y, count_z):
    blocks = split_axis(nodes, 2, count_z)
    blocks = split_axis(blocks, 1, count_y)
    return split_axis(blocks, 0, count_x)

def to_nodes(blocks, count_x, count_y, count_z):
    nodes = merge_axis(blocks, 0, count_x)
    nodes = merge_axis(nodes, 1, count_y)
    return merge_axis(nodes, 2, count_z)

def gradients_of(blocks, derivative):
    highest = lax.Precision.HIGHEST
    grad_x = jnp.einsum('sp,piqjrl->siqjrl', derivative, blocks, precision=highest)
    grad_y = jnp.einsum('sq,piqjrl->pisjrl', derivative, blocks, precision=highest)
    grad_z = jnp.einsum('sr,piqjrl->piqjsl', derivative, blocks, precision=highest)
    return (grad_x, grad_y, grad_z)

def element_force(blocks, element_stiff, derivative):
    highest = lax.Precision.HIGHEST
    grads = gradients_of(blocks, derivative)
    back = jnp.einsum('sp,siqjrl->piqjrl', derivative, element_stiff * grads[0], precision=highest)
    back = back + jnp.einsum('sq,pisjrl->piqjrl', derivative, element_stiff * grads[1], precision=highest)
    back = back + jnp.einsum('sr,piqjsl->piqjrl', derivative, element_stiff * grads[2], precision=highest)
    return (back, grads)

def inner_sum(first, second):
    return first[0] * second[0] + first[1] * second[1] + first[2] * second[2]

def reference(state_now, state_prev, adjoint_now, adjoint_next, modulus, density, receivers, observed):
    derivative, weights = gll_tables()
    weight_cube = cube_of(weights)
    element_stiff = weight_cube * modulus
    mass = density * line_weights(NX, 0)[:, None, None] * line_weights(NY, 0)[None, :, None] * line_weights(NZ, 0)[None, None, :]
    update_scale = TIME_STEP * TIME_STEP / mass
    owner = jnp.arange(RECEIVERS, dtype=jnp.int32) // REC_DEV
    plane_size = NY * NZ
    global_node = ((owner * (4 * EXD) + receivers // plane_size) * plane_size + receivers % plane_size).astype(jnp.int32)

    def global_blocks(nodal):
        return to_elements(jnp.pad(nodal, ((0, 1), (0, 1), (0, 1))), EX, EY, EZ)

    def global_force(nodal):
        forces, grads = element_force(global_blocks(nodal), element_stiff, derivative)
        return (to_nodes(forces, EX, EY, EZ)[:NX, :NY, :NZ], grads)

    def one_event(inputs):
        start_now, start_prev, adjoint_start, adjoint_after, observed_event = inputs

        def forward_step(state, unused):
            previous, current = state
            node_force, unused_grads = global_force(current)
            following = 2.0 * current - previous - update_scale * node_force
            return ((current, following), (current, following.reshape(-1)[global_node]))
        unused_state, (snapshots, records) = lax.scan(forward_step, (start_prev, start_now), None, length=NT)
        residual = records - observed_event
        energy = jnp.sum(observed_event * observed_event)
        misfit_sum = jnp.sum(residual * residual)
        mean_square = energy / (NT * RECEIVERS) + EPSILON
        misfit = 0.5 * misfit_sum / (NT * RECEIVERS * mean_square)
        sources = residual / mean_square

        def adjoint_step(state, inputs_step):
            adjoint_following, adjoint_current, accumulated = state
            snapshot, source = inputs_step
            node_force, adjoint_grads = global_force(adjoint_current)
            forward_grads = gradients_of(global_blocks(snapshot), derivative)
            accumulated = accumulated + inner_sum(forward_grads, adjoint_grads)
            injected = jnp.zeros((NX * NY * NZ,), jnp.float32).at[global_node].add(source).reshape(NX, NY, NZ)
            preceding = 2.0 * adjoint_current - adjoint_following + update_scale * (injected - node_force)
            return ((adjoint_current, preceding, accumulated), None)
        zero_total = jnp.zeros((5, EX, 5, EY, 5, EZ), jnp.float32)
        (unused_next, adjoint_last, accumulated), unused_out = lax.scan(adjoint_step, (adjoint_after, adjoint_start, zero_total), (snapshots[1:][::-1], sources[:NT - 1][::-1]))
        accumulated = accumulated + inner_sum(gradients_of(global_blocks(snapshots[0]), derivative), gradients_of(global_blocks(adjoint_last), derivative))
        return (-weight_cube * accumulated, misfit)
    kernels, misfits = lax.map(one_event, (state_now, state_prev, adjoint_now, adjoint_next, observed))
    summed = lax.optimization_barrier(jnp.sum(kernels, axis=0))
    largest = jnp.max(jnp.abs(summed))
    return (summed / (largest + EPSILON), misfits)
```

```python
from functools import partial
import math

import jax
import jax.numpy as jnp
import numpy as np
from jax import lax
from jax.experimental import pallas as pl
from jax.experimental.pallas import tpu as pltpu
from jax.sharding import PartitionSpec as P

TIME_STEP = 0.05
EPSILON = 1e-06
F32 = jnp.float32
BF16 = jnp.bfloat16


def gll_tables():
    root = math.sqrt(3.0 / 7.0)
    points = np.array([-1.0, -root, 0.0, root, 1.0])
    weights = np.array([0.1, 49.0 / 90.0, 32.0 / 45.0, 49.0 / 90.0, 0.1])
    legendre = (35.0 * points**4 - 30.0 * points**2 + 3.0) / 8.0
    derivative = np.zeros((5, 5))
    for row in range(5):
        for column in range(5):
            if row != column:
                derivative[row, column] = legendre[row] / (
                    legendre[column] * (points[row] - points[column])
                )
    derivative[0, 0] = -5.0
    derivative[4, 4] = 5.0
    return derivative, weights


DERIVATIVE, WEIGHTS = gll_tables()


def apply_line(matrix, u):
    e0, e1 = u[0] + u[4], u[1] + u[3]
    o0, o1 = u[0] - u[4], u[1] - u[3]
    out = [None] * 5
    for s in (0, 1):
        m = matrix[s]
        plus = float(0.5 * (m[0] - m[4])) * o0 + float(0.5 * (m[1] - m[3])) * o1
        minus = (
            float(0.5 * (m[0] + m[4])) * e0
            + float(0.5 * (m[1] + m[3])) * e1
            + float(m[2]) * u[2]
        )
        out[s] = plus + minus
        out[4 - s] = plus - minus
    out[2] = float(matrix[2][0]) * o0 + float(matrix[2][1]) * o1
    return out


def forward_line(u):
    return apply_line(DERIVATIVE, u)


def backward_line(h):
    return apply_line(DERIVATIVE.T, h)


def iotas():
    sub = lax.broadcasted_iota(jnp.int32, (8, 128), 0)
    lane = lax.broadcasted_iota(jnp.int32, (8, 128), 1)
    return sub, lane


def half_turn(v):
    return pltpu.roll(v, 4, 0)


class Shifts:
    def __init__(self):
        sub, lane = iotas()
        self.low = sub < 4
        self.row_first = (sub % 4) == 0
        self.row_last = (sub % 4) == 3
        self.lane_first = lane == 0
        self.lane_last = lane == 127

    def next_y(self, v):
        return jnp.where(self.row_last, 0.0, pltpu.roll(v, 7, 0))

    def next_z(self, v):
        return jnp.where(self.lane_last, 0.0, pltpu.roll(v, 127, 1))

    def carry_y(self, v):
        return jnp.where(self.row_first, 0.0, pltpu.roll(v, 1, 0))

    def carry_z(self, v):
        return jnp.where(self.lane_first, 0.0, pltpu.roll(v, 1, 1))


def pack_low(sh, halves):
    return [
        jnp.where(sh.low, halves[2 * k], half_turn(halves[2 * k + 1])) for k in range(8)
    ]


def pack_high(sh, halves):
    return [
        jnp.where(sh.low, half_turn(halves[2 * k]), halves[2 * k + 1]) for k in range(8)
    ]


def to_high(ref, base, qr):
    v = ref[base + qr // 2]
    return half_turn(v) if qr % 2 == 0 else v


def to_low(ref, base, qr):
    v = ref[base + qr // 2]
    return v if qr % 2 == 0 else half_turn(v)


def extended(sh, field, message, base):
    def get(p, qr):
        if p < 4:
            return field[p * 16 + qr]
        return jnp.where(sh.low, half_turn(field[qr]), to_high(message, base, qr))

    return get


def stored(field):
    def get(p, qr):
        return field[p * 16 + qr]

    return get


def expand(sh, get, blocks):
    for p in range(5):
        for r in range(4):
            for q in range(4):
                v = get(p, q * 4 + r)
                blocks[p * 25 + q * 5 + r] = v
                if r == 0:
                    blocks[p * 25 + q * 5 + 4] = sh.next_z(v)
                if q == 0:
                    far = sh.next_y(v)
                    blocks[p * 25 + 20 + r] = far
                    if r == 0:
                        blocks[p * 25 + 24] = sh.next_z(far)


def line_indices(direction, a, b):
    if direction == 0:
        return [k * 25 + a * 5 + b for k in range(5)]
    if direction == 1:
        return [a * 25 + k * 5 + b for k in range(5)]
    return [a * 25 + b * 5 + k for k in range(5)]


def force(sh, blocks, stiff, scratch, out):
    for q in range(5):
        for r in range(5):
            at = line_indices(0, q, r)
            g = forward_line([blocks[i] for i in at])
            f = backward_line([stiff[i] * g[k] for k, i in enumerate(at)])
            for k, i in enumerate(at):
                scratch[i] = f[k]
    for p in range(5):
        total = {}
        for q in range(5):
            at = line_indices(2, p, q)
            g = forward_line([blocks[i] for i in at])
            f = backward_line([stiff[i] * g[k] for k, i in enumerate(at)])
            for k, i in enumerate(at):
                total[i] = scratch[i] + f[k]
        for r in range(5):
            at = line_indices(1, p, r)
            g = forward_line([blocks[i] for i in at])
            f = backward_line([stiff[i] * g[k] for k, i in enumerate(at)])
            for k, i in enumerate(at):
                total[i] = total[i] + f[k]
        base = p * 25
        rows = {}
        for q in range(5):
            rows[q, 0] = total[base + q * 5] + sh.carry_z(total[base + q * 5 + 4])
            for r in range(1, 4):
                rows[q, r] = total[base + q * 5 + r]
        for r in range(4):
            out[p * 16 + r] = rows[0, r] + sh.carry_y(rows[4, r])
            for q in range(1, 4):
                out[p * 16 + q * 4 + r] = rows[q, r]


def products(first, second, acc, initial):
    for direction in range(3):
        for a in range(5):
            for b in range(5):
                at = line_indices(direction, a, b)
                g = forward_line([first[i] for i in at])
                h = forward_line([second[i] for i in at])
                for k, i in enumerate(at):
                    if initial and direction == 0:
                        acc[i] = g[k] * h[k]
                    else:
                        acc[i] = acc[i] + g[k] * h[k]


def assembled(sh, forces, from_left, left_base, from_right, right_base):
    def total(p, qr):
        f = forces[p * 16 + qr]
        if p == 0:
            return f + jnp.where(
                sh.low, to_low(from_left, left_base, qr), half_turn(forces[64 + qr])
            )
        if p == 4:
            return f + jnp.where(
                sh.low, half_turn(forces[qr]), to_high(from_right, right_base, qr)
            )
        return f

    return total


def put_messages(sh, forces, to_left, to_right, base):
    for k, v in enumerate(pack_low(sh, [forces[qr] for qr in range(16)])):
        to_left[base + k] = v
    for k, v in enumerate(pack_high(sh, [forces[64 + qr] for qr in range(16)])):
        to_right[base + k] = v


def split3(x):
    hi = x.astype(BF16)
    rest = x - hi.astype(F32)
    mid = rest.astype(BF16)
    lo = (rest - mid.astype(F32)).astype(BF16)
    return hi, mid, lo


def selection(swap):
    z = lax.broadcasted_iota(jnp.int32, (256, 256), 0)
    c = lax.broadcasted_iota(jnp.int32, (256, 256), 1)
    r = c // 64
    if swap:
        r = r + 1 - 2 * (r % 2)
    return jnp.where(z == 4 * (c % 64) + r, 1.0, 0.0).astype(BF16)


def to_local(x_ref, near, far, rows, emit):
    x = jnp.concatenate([x_ref[4 * i + p] for p in range(4) for i in range(2)], axis=0)
    first = second = None
    for part in split3(x):
        a = jnp.dot(part[:, :256], near, preferred_element_type=F32)
        b = jnp.dot(part[:, 256:], far, preferred_element_type=F32)
        first = a if first is None else first + a
        second = b if second is None else second + b
    lower = lax.broadcasted_iota(jnp.int32, (128, 128), 1) < 64
    for half in range(2):
        a = first[:, 128 * half : 128 * half + 128]
        b = second[:, 128 * half : 128 * half + 128]
        rows[2 * half] = jnp.where(lower, a, b)
        rows[2 * half + 1] = pltpu.roll(jnp.where(lower, b, a), 64, 1)
    for p in range(4):
        for q in range(4):
            for r in range(4):
                emit(p, q * 4 + r, rows[r, pl.ds(32 * p + q, 8, stride=4), :])


def first_kernel(now_ref, adjoint_ref, u_out, lam_out, message, rows):
    sh = Shifts()
    near, far = selection(False), selection(True)
    for which, (source, target) in enumerate(((now_ref, u_out), (adjoint_ref, lam_out))):

        def emit(p, qr, v, target=target):
            target[p * 16 + qr] = v

        to_local(source, near, far, rows, emit)
        for k, v in enumerate(pack_low(sh, [target[qr] for qr in range(16)])):
            message[8 * which + k] = v


def receiver_rows(receivers):
    x, yz = receivers // 8192, receivers % 8192
    y, z = yz // 512, yz % 512
    i, p, j, q, r = x // 4, x % 4, y // 4, y % 4, z % 4
    return ((p * 4 + q) * 4 + r) * 8 + i * 4 + j, z // 4


def one_hots(receivers):
    row, lane = receiver_rows(receivers)
    row_hot = lax.broadcasted_iota(jnp.int32, (512, 128), 0) == row
    lane_hot = lax.broadcasted_iota(jnp.int32, (128, 128), 0) == lane
    return row_hot, lane_hot


def second_kernel(
    slab_ref,
    prev_ref,
    next_ref,
    density_ref,
    modulus_ref,
    receivers_ref,
    observed_ref,
    prev_out,
    next_out,
    scale_out,
    stiff_out,
    counts_out,
    message,
    rows,
):
    sh = Shifts()
    sub, lane = iotas()
    near, far = selection(False), selection(True)
    for source, target in ((prev_ref, prev_out), (next_ref, next_out)):

        def emit(p, qr, v, target=target):
            target[p * 16 + qr] = v

        to_local(source, near, far, rows, emit)
    line = (0.2, 49.0 / 90.0, 32.0 / 45.0, 49.0 / 90.0)
    first_x = jnp.logical_and(sh.low, slab_ref[0] == 0)

    def emit_scale(p, qr, v):
        q, r = qr // 4, qr % 4
        mass = v * (jnp.where(first_x, 0.1, 0.2).astype(F32) if p == 0 else line[p])
        mass = mass * (jnp.where(sh.row_first, 0.1, 0.2).astype(F32) if q == 0 else line[q])
        mass = mass * (jnp.where(sh.lane_first, 0.1, 0.2).astype(F32) if r == 0 else line[r])
        scale_out[p * 16 + qr] = (TIME_STEP * TIME_STEP) / mass

    to_local(density_ref, near, far, rows, emit_scale)
    for p in range(5):
        for q in range(5):
            for r in range(5):
                weight = float(WEIGHTS[p] * WEIGHTS[q] * WEIGHTS[r])
                block = modulus_ref[p, :, q, :, r, :].reshape(8, 128)
                stiff_out[p * 25 + q * 5 + r] = weight * block
    row_hot, lane_hot = one_hots(receivers_ref[...])
    row_hot = jnp.where(row_hot, 1.0, 0.0).astype(BF16)
    ones = jnp.where(lane_hot, 1.0, 0.0)
    contract = (((1,), (1,)), ((), ()))

    def put_counts(which, total):
        for n in range(64):
            counts_out[which * 64 + n] = total[8 * n : 8 * n + 8]

    put_counts(
        0, lax.dot_general(row_hot, ones.astype(BF16), contract, preferred_element_type=F32)
    )
    for step in range(2):
        spread = jnp.where(lane_hot, observed_ref[step : step + 1, :], 0.0)
        total = None
        for part in split3(spread):
            t = lax.dot_general(row_hot, part, contract, preferred_element_type=F32)
            total = t if total is None else total + t
        put_counts(1 + step, total)
    sources = [(prev_out, 0), (next_out, 0), (scale_out, 0)]
    sources += [(counts_out, 0), (counts_out, 64), (counts_out, 128)]
    for which, (field, base) in enumerate(sources):
        for k, v in enumerate(pack_low(sh, [field[base + qr] for qr in range(16)])):
            message[8 * which + k] = v


def force_kernel(u_ref, lam_ref, message, stiff, u_force, lam_force, left, right, blocks, scratch):
    sh = Shifts()
    for which, (field, out) in enumerate(((u_ref, u_force), (lam_ref, lam_force))):
        expand(sh, extended(sh, field, message, 8 * which), blocks)
        force(sh, blocks, stiff, scratch, out)
        put_messages(sh, out, left, right, 8 * which)


def step_one_kernel(
    u_ref,
    lam_ref,
    prev_ref,
    next_ref,
    scale_ref,
    stiff,
    message0,
    message1,
    u_force,
    lam_force,
    from_left,
    from_right,
    u1_out,
    lam1_out,
    scale_out,
    u1_force,
    left,
    right,
    blocks,
    scratch,
):
    sh = Shifts()
    u0, lam2 = extended(sh, u_ref, message0, 0), extended(sh, lam_ref, message0, 8)
    before, after = extended(sh, prev_ref, message1, 0), extended(sh, next_ref, message1, 8)
    scale = extended(sh, scale_ref, message1, 16)
    u_total = assembled(sh, u_force, from_left, 0, from_right, 0)
    lam_total = assembled(sh, lam_force, from_left, 8, from_right, 8)
    for p in range(5):
        for qr in range(16):
            s = scale(p, qr)
            scale_out[p * 16 + qr] = s
            u1_out[p * 16 + qr] = 2.0 * u0(p, qr) - before(p, qr) - s * u_total(p, qr)
            lam1_out[p * 16 + qr] = 2.0 * lam2(p, qr) - after(p, qr) - s * lam_total(p, qr)
    expand(sh, stored(u1_out), blocks)
    force(sh, blocks, stiff, scratch, u1_force)
    put_messages(sh, u1_force, left, right, 0)


def step_two_kernel(
    square_ref,
    u_ref,
    message0,
    message1,
    u1_ref,
    lam1_ref,
    scale,
    counts,
    stiff,
    u1_force,
    from_left,
    from_right,
    u2_out,
    lam1_out,
    source_out,
    u2_force,
    lam1_force,
    left,
    right,
    blocks,
    scratch,
):
    sh = Shifts()
    inverse = 1.0 / square_ref[...]
    u0 = extended(sh, u_ref, message0, 0)
    count = extended(sh, counts.at[pl.ds(0, 64)], message1, 24)
    seen = [extended(sh, counts.at[pl.ds(64 + 64 * n, 64)], message1, 32 + 8 * n) for n in range(2)]
    total = assembled(sh, u1_force, from_left, 0, from_right, 0)
    for p in range(5):
        for qr in range(16):
            at = p * 16 + qr
            s, u1, c = scale[at], u1_ref[at], count(p, qr)
            u2 = 2.0 * u1 - u0(p, qr) - s * total(p, qr)
            u2_out[at] = u2
            lam1_out[at] = lam1_ref[at] + s * ((c * u2 - seen[1](p, qr)) * inverse)
            source_out[at] = s * ((c * u1 - seen[0](p, qr)) * inverse)
    expand(sh, stored(lam1_out), blocks)
    force(sh, blocks, stiff, scratch, lam1_force)
    put_messages(sh, lam1_force, left, right, 0)
    expand(sh, stored(u2_out), blocks)
    force(sh, blocks, stiff, scratch, u2_force)
    put_messages(sh, u2_force, left, right, 8)


def middle_kernel(u1_ref, lam1_ref, u2_ref, lam_ref, message0, acc, first, second):
    sh = Shifts()
    expand(sh, stored(u1_ref), first)
    expand(sh, stored(lam1_ref), second)
    products(first, second, acc, True)
    expand(sh, stored(u2_ref), first)
    expand(sh, extended(sh, lam_ref, message0, 8), second)
    products(first, second, acc, False)


def last_kernel(
    event_ref,
    u_ref,
    lam_ref,
    message0,
    lam1_ref,
    scale,
    source,
    lam1_force,
    from_left,
    from_right,
    acc_ref,
    out0,
    out1,
    out2,
    out3,
    lam0,
    first,
    second,
    acc,
    flat,
):
    sh = Shifts()
    lam2 = extended(sh, lam_ref, message0, 8)
    total = assembled(sh, lam1_force, from_left, 0, from_right, 0)
    for p in range(5):
        for qr in range(16):
            at = p * 16 + qr
            lam0[at] = (
                2.0 * lam1_ref[at] - lam2(p, qr) - scale[at] * total(p, qr) + source[at]
            )
    expand(sh, extended(sh, u_ref, message0, 0), first)
    expand(sh, stored(lam0), second)
    for i in range(125):
        acc[i] = acc_ref[i]
    products(first, second, acc, False)
    for p in range(5):
        for q in range(5):
            for r in range(5):
                at = p * 25 + q * 5 + r
                weight = float(-WEIGHTS[p] * WEIGHTS[q] * WEIGHTS[r])
                flat[8 * at : 8 * at + 8, :] = weight * acc[at]
    event = event_ref[0]
    for k, out in enumerate((out0, out1, out2, out3)):
        out[...] = flat[pl.ds((event + k) % 4, 250, stride=4), :]


def misfit_kernel(
    receivers_ref,
    observed_ref,
    u1_ref,
    u2_ref,
    scale,
    u2_force,
    from_left,
    from_right,
    out,
    u3,
):
    sh = Shifts()
    total = assembled(sh, u2_force, from_left, 8, from_right, 8)
    for p in range(4):
        for qr in range(16):
            at = p * 16 + qr
            u3[at] = 2.0 * u2_ref[at] - u1_ref[at] - scale[at] * total(p, qr)
    row_hot, lane_hot = one_hots(receivers_ref[...])
    row_hot = jnp.where(row_hot, 1.0, 0.0).astype(BF16)
    squares = jnp.zeros((1, 128), F32)
    for step, field in enumerate((u1_ref, u2_ref, u3)):
        values = field[pl.ds(0, 64)].reshape(512, 128)
        picked = None
        for part in split3(values):
            t = lax.dot_general(
                part, row_hot, (((0,), (0,)), ((), ())), preferred_element_type=F32
            )
            picked = t if picked is None else picked + t
        syn = jnp.sum(jnp.where(lane_hot, picked, 0.0), axis=0, keepdims=True)
        residual = syn - observed_ref[step : step + 1, :]
        squares = squares + residual * residual
    out[...] = jnp.broadcast_to(jnp.sum(squares, axis=1, keepdims=True), (1, 128))


def sum_kernel(a, b, c, d, misfit, total_out, message):
    total = a[...] + b[...] + c[...] + d[...]
    total_out[...] = total
    largest = jnp.max(jnp.max(jnp.abs(total), axis=0, keepdims=True), axis=1, keepdims=True)
    message[0:1, :] = jnp.broadcast_to(largest, (1, 128))
    message[1:2, :] = misfit[...]


def divide_kernel(total, message, out):
    inverse = jnp.broadcast_to(message[0:1, :] + EPSILON, (5, 128))
    for p in range(5):
        for i in range(2):
            for q in range(5):
                rows = total[pl.ds(2 * (25 * p + 5 * q) + i, 5, stride=2), :]
                out[p, i, q, 0] = rows / inverse


VMEM_SPEC = pl.BlockSpec(memory_space=pltpu.VMEM)
SMEM_SPEC = pl.BlockSpec(memory_space=pltpu.SMEM)


def call(kernel, args, outs, scratch=(), scalars=0, name=None):
    return pl.pallas_call(
        kernel,
        out_shape=[jax.ShapeDtypeStruct(shape, F32) for shape in outs],
        in_specs=[SMEM_SPEC] * scalars + [VMEM_SPEC] * (len(args) - scalars),
        out_specs=[VMEM_SPEC] * len(outs),
        scratch_shapes=[pltpu.VMEM(shape, F32) for shape in scratch],
        name=name or kernel.__name__,
    )(*args)


def vectors(count):
    return (count, 8, 128)


def neighbour(array, by):
    devices = lax.axis_size("space")
    pairs = [(i, i + by) for i in range(devices) if 0 <= i + by < devices]
    return lax.ppermute(array, "space", pairs)


def around(array, stride, size):
    devices = lax.axis_size("space")
    others = []
    for k in range(1, size):
        pairs = []
        for i in range(devices):
            c = (i // stride) % size
            pairs.append((i, i + (((c + k) % size) - c) * stride))
        others.append(lax.ppermute(array, "space", pairs))
    return others


def around_event(array_of):
    size = lax.axis_size("event")
    return [
        lax.ppermute(array_of(k), "event", [(i, (i + k) % size) for i in range(size)])
        for k in range(1, size)
    ]


def radices(devices):
    found, stride = [], 1
    while stride < devices:
        size = min(4, devices // stride)
        found.append((stride, size))
        stride *= size
    return found


def shards(state_now, state_prev, adjoint_now, adjoint_next, modulus, density, receivers, observed):
    slab = lax.axis_index("space").astype(jnp.int32).reshape(1)
    event = lax.axis_index("event").astype(jnp.int32).reshape(1)
    receivers = receivers.reshape(1, 128)
    observed = observed[0]
    stages = radices(lax.axis_size("space"))

    energy = jnp.broadcast_to(jnp.sum(observed * observed), (1, 128))

    u0, lam2, planes = call(
        first_kernel,
        (state_now[0], adjoint_now[0]),
        [vectors(64), vectors(64), vectors(16)],
        [(4, 128, 128)],
    )
    message0 = neighbour(planes, -1)
    before, after, scale, stiff, counts, planes = call(
        second_kernel,
        (slab, state_prev[0], adjoint_next[0], density, modulus, receivers, observed),
        [vectors(64), vectors(64), vectors(64), vectors(125), vectors(192), vectors(48)],
        [(4, 128, 128)],
        scalars=1,
    )
    message1 = neighbour(planes, -1)
    for stride, size in stages:
        energy = sum(around(energy, stride, size), energy)
    samples = 3 * 128 * lax.axis_size("space")
    mean_square = energy / samples + EPSILON

    u_force, lam_force, left, right = call(
        force_kernel,
        (u0, lam2, message0, stiff),
        [vectors(80), vectors(80), vectors(16), vectors(16)],
        [vectors(125), vectors(125)],
    )
    from_right, from_left = neighbour(left, -1), neighbour(right, 1)
    u1, lam1, scale, u1_force, left, right = call(
        step_one_kernel,
        (
            u0,
            lam2,
            before,
            after,
            scale,
            stiff,
            message0,
            message1,
            u_force,
            lam_force,
            from_left,
            from_right,
        ),
        [vectors(80)] * 4 + [vectors(8)] * 2,
        [vectors(125), vectors(125)],
    )
    from_right, from_left = neighbour(left, -1), neighbour(right, 1)
    u2, lam1, source, u2_force, lam1_force, left, right = call(
        step_two_kernel,
        (
            mean_square,
            u0,
            message0,
            message1,
            u1,
            lam1,
            scale,
            counts,
            stiff,
            u1_force,
            from_left,
            from_right,
        ),
        [vectors(80)] * 5 + [vectors(16)] * 2,
        [vectors(125), vectors(125)],
    )
    from_right, from_left = neighbour(left, -1), neighbour(right, 1)
    (acc,) = call(
        middle_kernel,
        (u1, lam1, u2, lam2, message0),
        [vectors(125)],
        [vectors(125), vectors(125)],
    )
    pieces = call(
        last_kernel,
        (
            event,
            u0,
            lam2,
            message0,
            lam1,
            scale,
            source,
            lam1_force,
            from_left,
            from_right,
            acc,
        ),
        [(250, 128)] * 4,
        [vectors(80), vectors(125), vectors(125), vectors(125), (1000, 128)],
        scalars=1,
    )
    others = around_event(lambda k: pieces[k])
    (squares,) = call(
        misfit_kernel,
        (receivers, observed, u1, u2, scale, u2_force, from_left, from_right),
        [(1, 128)],
        [vectors(64)],
    )
    total, message = call(
        sum_kernel, (pieces[0], *others, squares), [(250, 128), (2, 128)]
    )
    largest, squares = message[0:1], message[1:2]
    is_first = lax.broadcasted_iota(jnp.int32, (2, 128), 0) == 0
    for stride, size in stages:
        others = around(message, stride, size)
        top, sums = message, message
        for other in others:
            top, sums = jnp.maximum(top, other), sums + other
        message = jnp.where(is_first, top, sums)
    misfit = 0.5 * message[1, :1] / (samples * mean_square[0, :1])
    others = around_event(lambda k: message)
    for other in others:
        message = jnp.maximum(message, other)
    (kernel,) = call(divide_kernel, (total, message), [(5, 2, 5, 1, 5, 128)])
    return (kernel, misfit)


def solution(mesh):
    in_specs = (
        P("event", "space", None, None),
        P("event", "space", None, None),
        P("event", "space", None, None),
        P("event", "space", None, None),
        P(None, "space", None, None, None, None),
        P("space", None, None),
        P("space"),
        P("event", None, "space"),
    )
    out_specs = (P(None, "space", None, "event", None, None), P("event"))
    return jax.shard_map(shards, mesh=mesh, in_specs=in_specs, out_specs=out_specs, check_vma=False)
```

```python
import math

import jax
import jax.numpy as jnp
import numpy as np
from jax import lax
from jax.experimental import pallas as pl
from jax.experimental.pallas import tpu as pltpu
from jax.sharding import PartitionSpec as P


TIME_STEP = 0.05
EPSILON = 1e-06
F32 = jnp.float32
BF16 = jnp.bfloat16
SAMPLES = 24576


def gll_tables():
    root = math.sqrt(3.0 / 7.0)
    points = np.array([-1.0, -root, 0.0, root, 1.0])
    weights = np.array([0.1, 49.0 / 90.0, 32.0 / 45.0, 49.0 / 90.0, 0.1])
    legendre = (35.0 * points**4 - 30.0 * points**2 + 3.0) / 8.0
    derivative = np.zeros((5, 5))
    for row in range(5):
        for column in range(5):
            if row != column:
                derivative[row, column] = legendre[row] / (
                    legendre[column] * (points[row] - points[column])
                )
    derivative[0, 0] = -5.0
    derivative[4, 4] = 5.0
    return derivative, weights


DERIVATIVE, WEIGHTS = gll_tables()


def apply_line(matrix, u):
    e0, e1 = u[0] + u[4], u[1] + u[3]
    o0, o1 = u[0] - u[4], u[1] - u[3]
    out = [None] * 5
    for s in (0, 1):
        m = matrix[s]
        plus = float(0.5 * (m[0] - m[4])) * o0 + float(0.5 * (m[1] - m[3])) * o1
        minus = (
            float(0.5 * (m[0] + m[4])) * e0
            + float(0.5 * (m[1] + m[3])) * e1
            + float(m[2]) * u[2]
        )
        out[s] = plus + minus
        out[4 - s] = plus - minus
    out[2] = float(matrix[2][0]) * o0 + float(matrix[2][1]) * o1
    return out


def forward_line(u):
    return apply_line(DERIVATIVE, u)


def backward_line(h):
    return apply_line(DERIVATIVE.T, h)


def iotas():
    sub = lax.broadcasted_iota(jnp.int32, (8, 128), 0)
    lane = lax.broadcasted_iota(jnp.int32, (8, 128), 1)
    return sub, lane


def half_turn(v):
    return pltpu.roll(v, 4, 0)


class Shifts:
    def __init__(self):
        sub, lane = iotas()
        self.low = sub < 4
        self.row_first = (sub % 4) == 0
        self.row_last = (sub % 4) == 3
        self.lane_first = lane == 0
        self.lane_last = lane == 127

    def next_y(self, v):
        return jnp.where(self.row_last, 0.0, pltpu.roll(v, 7, 0))

    def next_z(self, v):
        return jnp.where(self.lane_last, 0.0, pltpu.roll(v, 127, 1))

    def carry_y(self, v):
        return jnp.where(self.row_first, 0.0, pltpu.roll(v, 1, 0))

    def carry_z(self, v):
        return jnp.where(self.lane_first, 0.0, pltpu.roll(v, 1, 1))


def pack_low(sh, halves):
    return [
        jnp.where(sh.low, halves[2 * k], half_turn(halves[2 * k + 1])) for k in range(8)
    ]


def pack_high(sh, halves):
    return [
        jnp.where(sh.low, half_turn(halves[2 * k]), halves[2 * k + 1]) for k in range(8)
    ]


def to_high(ref, base, qr):
    v = ref[base + qr // 2]
    return half_turn(v) if qr % 2 == 0 else v


def extended(sh, field, message, base):
    def get(p, qr):
        if p < 4:
            return field[p * 16 + qr]
        return jnp.where(sh.low, half_turn(field[qr]), to_high(message, base, qr))

    return get


def stored(field):
    def get(p, qr):
        return field[p * 16 + qr]

    return get


def expand(sh, get, blocks):
    for p in range(5):
        for r in range(4):
            for q in range(4):
                v = get(p, q * 4 + r)
                blocks[p * 25 + q * 5 + r] = v
                if r == 0:
                    blocks[p * 25 + q * 5 + 4] = sh.next_z(v)
                if q == 0:
                    far = sh.next_y(v)
                    blocks[p * 25 + 20 + r] = far
                    if r == 0:
                        blocks[p * 25 + 24] = sh.next_z(far)


def line_indices(direction, a, b):
    if direction == 0:
        return [k * 25 + a * 5 + b for k in range(5)]
    if direction == 1:
        return [a * 25 + k * 5 + b for k in range(5)]
    return [a * 25 + b * 5 + k for k in range(5)]


def force(sh, blocks, stiff, scratch, out):
    for q in range(5):
        for r in range(5):
            at = line_indices(0, q, r)
            g = forward_line([blocks[i] for i in at])
            f = backward_line([stiff[i] * g[k] for k, i in enumerate(at)])
            for k, i in enumerate(at):
                scratch[i] = f[k]
    for p in range(5):
        total = {}
        for q in range(5):
            at = line_indices(2, p, q)
            g = forward_line([blocks[i] for i in at])
            f = backward_line([stiff[i] * g[k] for k, i in enumerate(at)])
            for k, i in enumerate(at):
                total[i] = scratch[i] + f[k]
        for r in range(5):
            at = line_indices(1, p, r)
            g = forward_line([blocks[i] for i in at])
            f = backward_line([stiff[i] * g[k] for k, i in enumerate(at)])
            for k, i in enumerate(at):
                total[i] = total[i] + f[k]
        for qr, v in enumerate(assemble(sh, [total[p * 25 + n] for n in range(25)])):
            out[p * 16 + qr] = v


def assemble(sh, face):
    rows = {}
    for q in range(5):
        rows[q, 0] = face[q * 5] + sh.carry_z(face[q * 5 + 4])
        for r in range(1, 4):
            rows[q, r] = face[q * 5 + r]
    nodes = []
    for q in range(4):
        for r in range(4):
            nodes.append(rows[0, r] + sh.carry_y(rows[4, r]) if q == 0 else rows[q, r])
    return nodes


def products(first, second, acc, initial):
    for direction in range(3):
        for a in range(5):
            for b in range(5):
                at = line_indices(direction, a, b)
                g = forward_line([first[i] for i in at])
                h = forward_line([second[i] for i in at])
                for k, i in enumerate(at):
                    if initial and direction == 0:
                        acc[i] = g[k] * h[k]
                    else:
                        acc[i] = acc[i] + g[k] * h[k]


def assembled(sh, forces, incoming, base):
    def total(p, qr):
        f = forces[p * 16 + qr]
        if p == 0:
            return f + jnp.where(
                sh.low, incoming.from_left(base, qr), half_turn(forces[64 + qr])
            )
        if p == 4:
            return f + jnp.where(
                sh.low, half_turn(forces[qr]), incoming.from_right(base, qr)
            )
        return f

    return total


def put_messages(sh, odd, forces, far, near, base):
    to_left = pack_low(sh, [forces[qr] for qr in range(16)])
    to_right = pack_high(sh, [forces[64 + qr] for qr in range(16)])
    for k in range(8):
        far[base + k] = jnp.where(odd, to_right[k], to_left[k])
        near[base + k] = jnp.where(odd, to_left[k], to_right[k])


class Incoming:
    def __init__(self, odd, far, near):
        self.odd, self.far, self.near = odd, far, near

    def from_left(self, base, qr):
        at = base + qr // 2
        v = jnp.where(self.odd, self.near[at], self.far[at])
        return v if qr % 2 == 0 else half_turn(v)

    def from_right(self, base, qr):
        at = base + qr // 2
        v = jnp.where(self.odd, self.far[at], self.near[at])
        return half_turn(v) if qr % 2 == 0 else v


def is_odd(slab_ref):
    return slab_ref[0] % 2 == 1


def split3(x):
    hi = x.astype(BF16)
    rest = x - hi.astype(F32)
    mid = rest.astype(BF16)
    lo = (rest - mid.astype(F32)).astype(BF16)
    return hi, mid, lo


def selection(swap):
    z = lax.broadcasted_iota(jnp.int32, (256, 256), 0)
    c = lax.broadcasted_iota(jnp.int32, (256, 256), 1)
    r = c // 64
    if swap:
        r = r + 1 - 2 * (r % 2)
    return jnp.where(z == 4 * (c % 64) + r, 1.0, 0.0).astype(BF16)


def to_local(x_ref, near, far, rows, emit):
    x = jnp.concatenate([x_ref[4 * i + p] for p in range(4) for i in range(2)], axis=0)
    first = second = None
    for part in split3(x):
        a = jnp.dot(part[:, :256], near, preferred_element_type=F32)
        b = jnp.dot(part[:, 256:], far, preferred_element_type=F32)
        first = a if first is None else first + a
        second = b if second is None else second + b
    lower = lax.broadcasted_iota(jnp.int32, (128, 128), 1) < 64
    for half in range(2):
        a = first[:, 128 * half : 128 * half + 128]
        b = second[:, 128 * half : 128 * half + 128]
        rows[2 * half] = jnp.where(lower, a, b)
        rows[2 * half + 1] = pltpu.roll(jnp.where(lower, b, a), 64, 1)
    for p in range(4):
        for q in range(4):
            for r in range(4):
                emit(p, q * 4 + r, rows[r, pl.ds(32 * p + q, 8, stride=4), :])


def load(sources, buffers, semaphores):
    copies = [
        pltpu.make_async_copy(source, buffer, semaphores.at[k])
        for k, (source, buffer) in enumerate(zip(sources, buffers))
    ]
    for copy in copies:
        copy.start()
    return copies


def first_kernel(
    now_hbm, adjoint_hbm, u_out, lam_out, message, rows, now_ref, adjoint_ref, semaphores
):
    copies = load((now_hbm, adjoint_hbm), (now_ref, adjoint_ref), semaphores)
    sh = Shifts()
    near, far = selection(False), selection(True)
    for which, (source, target) in enumerate(((now_ref, u_out), (adjoint_ref, lam_out))):

        def emit(p, qr, v, target=target):
            target[p * 16 + qr] = v

        copies[which].wait()
        to_local(source, near, far, rows, emit)
        for k, v in enumerate(pack_low(sh, [target[qr] for qr in range(16)])):
            message[8 * which + k] = v


def receiver_rows(receivers):
    x, yz = receivers // 8192, receivers % 8192
    y, z = yz // 512, yz % 512
    i, p, j, q, r = x // 4, x % 4, y // 4, y % 4, z % 4
    return ((p * 4 + q) * 4 + r) * 8 + i * 4 + j, z // 4


def one_hots(receivers):
    row, lane = receiver_rows(receivers)
    row_hot = lax.broadcasted_iota(jnp.int32, (512, 128), 0) == row
    lane_hot = lax.broadcasted_iota(jnp.int32, (128, 128), 0) == lane
    return row_hot, lane_hot


def second_kernel(
    slab_ref,
    prev_hbm,
    next_hbm,
    density_hbm,
    modulus_hbm,
    receivers_ref,
    observed_ref,
    prev_out,
    next_out,
    scale_out,
    stiff_out,
    counts_out,
    message,
    rows,
    prev_ref,
    next_ref,
    density_ref,
    modulus_ref,
    semaphores,
):
    copies = load(
        (prev_hbm, next_hbm, density_hbm, modulus_hbm),
        (prev_ref, next_ref, density_ref, modulus_ref),
        semaphores,
    )
    sh = Shifts()
    sub, lane = iotas()
    near, far = selection(False), selection(True)
    for which, (source, target) in enumerate(((prev_ref, prev_out), (next_ref, next_out))):

        def emit(p, qr, v, target=target):
            target[p * 16 + qr] = v

        copies[which].wait()
        to_local(source, near, far, rows, emit)
    line = (0.2, 49.0 / 90.0, 32.0 / 45.0, 49.0 / 90.0)
    first_x = jnp.logical_and(sh.low, slab_ref[0] == 0)

    def emit_scale(p, qr, v):
        q, r = qr // 4, qr % 4
        mass = v * (jnp.where(first_x, 0.1, 0.2).astype(F32) if p == 0 else line[p])
        mass = mass * (jnp.where(sh.row_first, 0.1, 0.2).astype(F32) if q == 0 else line[q])
        mass = mass * (jnp.where(sh.lane_first, 0.1, 0.2).astype(F32) if r == 0 else line[r])
        scale_out[p * 16 + qr] = (TIME_STEP * TIME_STEP) / mass

    copies[2].wait()
    to_local(density_ref, near, far, rows, emit_scale)
    copies[3].wait()
    for p in range(5):
        for q in range(5):
            for r in range(5):
                weight = float(WEIGHTS[p] * WEIGHTS[q] * WEIGHTS[r])
                block = jnp.concatenate(
                    [modulus_ref[p, 0, q, r], modulus_ref[p, 1, q, r]], axis=0
                )
                stiff_out[p * 25 + q * 5 + r] = weight * block
    row_hot, lane_hot = one_hots(receivers_ref[...])
    row_hot = jnp.where(row_hot, 1.0, 0.0).astype(BF16)
    ones = jnp.where(lane_hot, 1.0, 0.0)
    contract = (((1,), (1,)), ((), ()))

    def put_counts(which, total):
        for n in range(64):
            counts_out[which * 64 + n] = total[8 * n : 8 * n + 8]

    put_counts(
        0, lax.dot_general(row_hot, ones.astype(BF16), contract, preferred_element_type=F32)
    )
    for step in range(2):
        spread = jnp.where(lane_hot, observed_ref[step], 0.0)
        total = None
        for part in split3(spread):
            t = lax.dot_general(row_hot, part, contract, preferred_element_type=F32)
            total = t if total is None else total + t
        put_counts(1 + step, total)
    sources = [(prev_out, 0), (next_out, 0), (scale_out, 0)]
    sources += [(counts_out, 0), (counts_out, 64), (counts_out, 128)]
    for which, (field, base) in enumerate(sources):
        for k, v in enumerate(pack_low(sh, [field[base + qr] for qr in range(16)])):
            message[8 * which + k] = v


def without_far(sh, field):
    def get(p, qr):
        if p < 4:
            return field[p * 16 + qr]
        return jnp.where(sh.low, half_turn(field[qr]), 0.0)

    return get


def force_kernel(u_ref, lam_ref, stiff, u_force, lam_force, blocks, scratch):
    sh = Shifts()
    for field, out in ((u_ref, u_force), (lam_ref, lam_force)):
        expand(sh, without_far(sh, field), blocks)
        force(sh, blocks, stiff, scratch, out)


def far_plane_kernel(
    slab_ref, message, stiff, u_in, lam_in, u_force, lam_force, far, near, column
):
    sh = Shifts()
    odd = is_odd(slab_ref)
    for n in range(25):
        f = backward_line([float(DERIVATIVE[k, 4]) * stiff[k * 25 + n] for k in range(5)])
        for k in range(5):
            column[k * 25 + n] = f[k]
    for which, (source, out) in enumerate(((u_in, u_force), (lam_in, lam_force))):
        face = [None] * 25
        for q in range(4):
            for r in range(4):
                v = jnp.where(sh.low, 0.0, to_high(message, 8 * which, q * 4 + r))
                face[q * 5 + r] = v
                if r == 0:
                    face[q * 5 + 4] = sh.next_z(v)
                if q == 0:
                    face[20 + r] = sh.next_y(v)
                    if r == 0:
                        face[24] = sh.next_z(face[20])
        for p in range(5):
            added = [column[p * 25 + n] * face[n] for n in range(25)]
            if p == 4:
                for a in range(5):
                    for at in ([a * 5 + k for k in range(5)], [k * 5 + a for k in range(5)]):
                        g = forward_line([face[n] for n in at])
                        f = backward_line([stiff[100 + n] * g[k] for k, n in enumerate(at)])
                        for k, n in enumerate(at):
                            added[n] = added[n] + f[k]
            for qr, v in enumerate(assemble(sh, added)):
                out[p * 16 + qr] = source[p * 16 + qr] + v
        put_messages(sh, odd, out, far, near, 8 * which)


def step_one_kernel(
    slab_ref,
    u_ref,
    lam_ref,
    prev_ref,
    next_ref,
    scale_ref,
    stiff,
    message0,
    message1,
    u_force,
    lam_force,
    far_in,
    near_in,
    u1_out,
    lam1_out,
    scale_out,
    u1_force,
    far,
    near,
    blocks,
    scratch,
):
    sh = Shifts()
    odd = is_odd(slab_ref)
    incoming = Incoming(odd, far_in, near_in)
    u0, lam2 = extended(sh, u_ref, message0, 0), extended(sh, lam_ref, message0, 8)
    before, after = extended(sh, prev_ref, message1, 0), extended(sh, next_ref, message1, 8)
    scale = extended(sh, scale_ref, message1, 16)
    u_total = assembled(sh, u_force, incoming, 0)
    lam_total = assembled(sh, lam_force, incoming, 8)
    for p in range(5):
        for qr in range(16):
            s = scale(p, qr)
            scale_out[p * 16 + qr] = s
            u1_out[p * 16 + qr] = 2.0 * u0(p, qr) - before(p, qr) - s * u_total(p, qr)
            lam1_out[p * 16 + qr] = 2.0 * lam2(p, qr) - after(p, qr) - s * lam_total(p, qr)
    expand(sh, stored(u1_out), blocks)
    force(sh, blocks, stiff, scratch, u1_force)
    put_messages(sh, odd, u1_force, far, near, 0)


def mean_square(energy):
    total = jnp.sum(energy, axis=1, keepdims=True)
    return total / SAMPLES + EPSILON


def step_two_kernel(
    slab_ref,
    energy_ref,
    u_ref,
    message0,
    message1,
    u1_ref,
    lam1_ref,
    scale,
    counts,
    stiff,
    u1_force,
    far_in,
    near_in,
    u2_out,
    lam1_out,
    source_out,
    u2_force,
    lam1_force,
    far,
    near,
    blocks,
    scratch,
):
    sh = Shifts()
    odd = is_odd(slab_ref)
    incoming = Incoming(odd, far_in, near_in)
    inverse = jnp.broadcast_to(1.0 / mean_square(energy_ref[...]), (8, 128))
    u0 = extended(sh, u_ref, message0, 0)
    count = extended(sh, counts.at[pl.ds(0, 64)], message1, 24)
    seen = [extended(sh, counts.at[pl.ds(64 + 64 * n, 64)], message1, 32 + 8 * n) for n in range(2)]
    total = assembled(sh, u1_force, incoming, 0)
    for p in range(5):
        for qr in range(16):
            at = p * 16 + qr
            s, u1, c = scale[at], u1_ref[at], count(p, qr)
            u2 = 2.0 * u1 - u0(p, qr) - s * total(p, qr)
            u2_out[at] = u2
            lam1_out[at] = lam1_ref[at] + s * ((c * u2 - seen[1](p, qr)) * inverse)
            source_out[at] = s * ((c * u1 - seen[0](p, qr)) * inverse)
    expand(sh, stored(lam1_out), blocks)
    force(sh, blocks, stiff, scratch, lam1_force)
    put_messages(sh, odd, lam1_force, far, near, 0)
    expand(sh, stored(u2_out), blocks)
    force(sh, blocks, stiff, scratch, u2_force)
    put_messages(sh, odd, u2_force, far, near, 8)


def middle_kernel(u1_ref, lam1_ref, u2_ref, lam_ref, message0, acc, first, second):
    sh = Shifts()
    expand(sh, stored(u1_ref), first)
    expand(sh, stored(lam1_ref), second)
    products(first, second, acc, True)
    expand(sh, stored(u2_ref), first)
    expand(sh, extended(sh, lam_ref, message0, 8), second)
    products(first, second, acc, False)


def last_kernel(
    slab_ref,
    event_ref,
    u_ref,
    lam_ref,
    message0,
    lam1_ref,
    scale,
    source,
    lam1_force,
    far_in,
    near_in,
    acc_ref,
    out0,
    out1,
    out2,
    out3,
    lam0,
    first,
    second,
    acc,
    flat,
):
    sh = Shifts()
    lam2 = extended(sh, lam_ref, message0, 8)
    total = assembled(sh, lam1_force, Incoming(is_odd(slab_ref), far_in, near_in), 0)
    for p in range(5):
        for qr in range(16):
            at = p * 16 + qr
            lam0[at] = (
                2.0 * lam1_ref[at] - lam2(p, qr) - scale[at] * total(p, qr) + source[at]
            )
    expand(sh, extended(sh, u_ref, message0, 0), first)
    expand(sh, stored(lam0), second)
    for i in range(125):
        acc[i] = acc_ref[i]
    products(first, second, acc, False)
    for p in range(5):
        for q in range(5):
            for r in range(5):
                at = p * 25 + q * 5 + r
                weight = float(-WEIGHTS[p] * WEIGHTS[q] * WEIGHTS[r])
                v = weight * acc[at]
                for i in range(2):
                    row = 4 * ((2 * p + i) * 25 + q * 5 + r)
                    flat[row : row + 4, :] = v[4 * i : 4 * i + 4]
    event = event_ref[0]
    for k, out in enumerate((out0, out1, out2, out3)):
        out[...] = flat[pl.ds(jnp.bitwise_xor(event, k), 250, stride=4), :]


def misfit_kernel(
    slab_ref,
    receivers_ref,
    observed_ref,
    u1_ref,
    u2_ref,
    scale,
    u2_force,
    far_in,
    near_in,
    out,
    u3,
):
    sh = Shifts()
    total = assembled(sh, u2_force, Incoming(is_odd(slab_ref), far_in, near_in), 8)
    for p in range(4):
        for qr in range(16):
            at = p * 16 + qr
            u3[at] = 2.0 * u2_ref[at] - u1_ref[at] - scale[at] * total(p, qr)
    row_hot, lane_hot = one_hots(receivers_ref[...])
    row_hot = jnp.where(row_hot, 1.0, 0.0).astype(BF16)
    squares = jnp.zeros((1, 128), F32)
    for step, field in enumerate((u1_ref, u2_ref, u3)):
        values = field[pl.ds(0, 64)].reshape(512, 128)
        picked = None
        for part in split3(values):
            t = lax.dot_general(
                part, row_hot, (((0,), (0,)), ((), ())), preferred_element_type=F32
            )
            picked = t if picked is None else picked + t
        syn = jnp.sum(jnp.where(lane_hot, picked, 0.0), axis=0, keepdims=True)
        residual = syn - observed_ref[step]
        squares = squares + residual * residual
    out[...] = jnp.broadcast_to(jnp.sum(squares, axis=1, keepdims=True), (1, 128))


def sum_kernel(a, b, c, d, misfit, total_out, message):
    total = a[...] + b[...] + c[...] + d[...]
    total_out[...] = total
    largest = jnp.max(jnp.max(jnp.abs(total), axis=0, keepdims=True), axis=1, keepdims=True)
    first_half = lax.broadcasted_iota(jnp.int32, (1, 128), 1) < 64
    message[...] = jnp.where(first_half, jnp.broadcast_to(largest, (1, 128)), misfit[...])


def divide_kernel(event_ref, total, gathered, energy_ref, out, misfit_out):
    rows = gathered[...]
    first_half = lax.broadcasted_iota(jnp.int32, (1, 128), 1) < 64
    top = jnp.where(first_half, jnp.max(rows, axis=0, keepdims=True), 0.0)
    largest = jnp.max(top, axis=1, keepdims=True)
    spaces = gathered.shape[0] // 4
    mine = gathered[pl.ds(pl.multiple_of(event_ref[0] * spaces, spaces), spaces), :]
    squares = jnp.where(first_half, 0.0, jnp.sum(mine, axis=0, keepdims=True))
    squares = jnp.max(squares, axis=1, keepdims=True)
    misfit_out[...] = jnp.broadcast_to(
        0.5 * squares / (SAMPLES * mean_square(energy_ref[...])), (1, 128)
    )
    out[...] = (total[...] / (largest + EPSILON)).reshape(250, 1, 128)


COST = 16 << 20
VMEM_GRANT = 16 << 20
VMEM_SPEC = pl.BlockSpec(memory_space=pltpu.VMEM)
HBM_SPEC = pl.BlockSpec(memory_space=pltpu.MemorySpace.HBM)
SMEM_SPEC = pl.BlockSpec(memory_space=pltpu.SMEM)


def call(kernel, args, outs, scratch=(), scalars=0, loads=0):
    buffers = [pltpu.VMEM(arg.shape, F32) for arg in args[scalars : scalars + loads]]
    semaphores = [pltpu.SemaphoreType.DMA((loads,))] if loads else []
    return pl.pallas_call(
        kernel,
        out_shape=[jax.ShapeDtypeStruct(shape, F32) for shape in outs],
        in_specs=[SMEM_SPEC] * scalars
        + [HBM_SPEC] * loads
        + [VMEM_SPEC] * (len(args) - scalars - loads),
        out_specs=[VMEM_SPEC] * len(outs),
        scratch_shapes=[pltpu.VMEM(shape, F32) for shape in scratch] + buffers + semaphores,
        cost_estimate=pl.CostEstimate(flops=0, bytes_accessed=COST, transcendentals=0),
        compiler_params=pltpu.CompilerParams(vmem_limit_bytes=VMEM_GRANT),
    )(*args)


def vectors(count):
    return (count, 8, 128)


def to_left(array):
    devices = lax.axis_size("space")
    return lax.ppermute(array, "space", [(i, i - 1) for i in range(1, devices)])


def exchange(far, near):
    devices = lax.axis_size("space")
    far_pairs = [(i, i + 1 if i % 2 else i - 1) for i in range(1, devices - 1)]
    near_pairs = [(i, i - 1 if i % 2 else i + 1) for i in range(devices)]
    return (lax.ppermute(far, "space", far_pairs), lax.ppermute(near, "space", near_pairs))


def across(array, stride):
    devices = lax.axis_size("space")
    return array + lax.ppermute(array, "space", [(i, i ^ stride) for i in range(devices)])


def shards(state_now, state_prev, adjoint_now, adjoint_next, modulus, density, receivers, observed):
    slab = lax.axis_index("space").astype(jnp.int32).reshape(1)
    event = lax.axis_index("event").astype(jnp.int32).reshape(1)
    receivers = receivers.reshape(1, 128)
    observed = jnp.transpose(observed, (1, 0, 2))
    modulus = jnp.transpose(modulus, (0, 1, 2, 4, 3, 5))

    energy = jnp.sum(observed * observed, axis=0)
    energy = across(energy, 1)

    u0, lam2, planes = call(
        first_kernel,
        (state_now[0], adjoint_now[0]),
        [vectors(64), vectors(64), vectors(16)],
        [(4, 128, 128)],
        loads=2,
    )
    energy = across(energy, 16)
    message0 = to_left(planes)
    before, after, scale, stiff, counts, planes = call(
        second_kernel,
        (slab, state_prev[0], adjoint_next[0], density, modulus, receivers, observed),
        [vectors(64), vectors(64), vectors(64), vectors(125), vectors(192), vectors(48)],
        [(4, 128, 128)],
        scalars=1,
        loads=4,
    )
    energy = across(energy, 2)
    message1 = to_left(planes)
    u_force, lam_force = call(
        force_kernel,
        (u0, lam2, stiff),
        [vectors(80), vectors(80)],
        [vectors(125), vectors(125)],
    )
    energy = across(energy, 32)
    u_force, lam_force, far, near = call(
        far_plane_kernel,
        (slab, message0, stiff, u_force, lam_force),
        [vectors(80), vectors(80), vectors(16), vectors(16)],
        [vectors(125)],
        scalars=1,
    )
    energy = across(energy, 4)
    far, near = exchange(far, near)
    u1, lam1, scale, u1_force, far, near = call(
        step_one_kernel,
        (
            slab,
            u0,
            lam2,
            before,
            after,
            scale,
            stiff,
            message0,
            message1,
            u_force,
            lam_force,
            far,
            near,
        ),
        [vectors(80)] * 4 + [vectors(8)] * 2,
        [vectors(125), vectors(125)],
        scalars=1,
    )
    energy = across(energy, 8)
    far, near = exchange(far, near)
    u2, lam1, source, u2_force, lam1_force, far, near = call(
        step_two_kernel,
        (
            slab,
            energy,
            u0,
            message0,
            message1,
            u1,
            lam1,
            scale,
            counts,
            stiff,
            u1_force,
            far,
            near,
        ),
        [vectors(80)] * 5 + [vectors(16)] * 2,
        [vectors(125), vectors(125)],
        scalars=1,
    )
    far, near = exchange(far, near)
    (acc,) = call(
        middle_kernel,
        (u1, lam1, u2, lam2, message0),
        [vectors(125)],
        [vectors(125), vectors(125)],
    )
    pieces = call(
        last_kernel,
        (slab, event, u0, lam2, message0, lam1, scale, source, lam1_force, far, near, acc),
        [(250, 128)] * 4,
        [vectors(80), vectors(125), vectors(125), vectors(125), (1000, 128)],
        scalars=2,
    )
    events = lax.axis_size("event")
    others = [
        lax.ppermute(pieces[k], "event", [(i, i ^ k) for i in range(events)])
        for k in (1, 2, 3)
    ]
    (squares,) = call(
        misfit_kernel,
        (slab, receivers, observed, u1, u2, scale, u2_force, far, near),
        [(1, 128)],
        [vectors(64)],
        scalars=1,
    )
    total, message = call(
        sum_kernel, (pieces[0], *others, squares), [(250, 128), (1, 128)]
    )
    everyone = ("event", "space")
    devices = lax.axis_size("event") * lax.axis_size("space")
    gathered = lax.all_to_all(
        jnp.broadcast_to(message[None], (devices, 1, 128)), everyone, 0, 0
    )
    kernel, misfit = call(
        divide_kernel,
        (event, total, gathered.reshape(devices, 128), energy),
        [(250, 1, 128), (1, 128)],
        scalars=1,
    )
    kernel = jnp.transpose(kernel.reshape(5, 2, 5, 5, 1, 128), (0, 1, 2, 4, 3, 5))
    return (kernel, misfit[0, :1])


def solution(mesh):
    in_specs = (
        P("event", "space", None, None),
        P("event", "space", None, None),
        P("event", "space", None, None),
        P("event", "space", None, None),
        P(None, "space", None, None, None, None),
        P("space", None, None),
        P("space"),
        P("event", None, "space"),
    )
    out_specs = (P(None, "space", None, "event", None, None), P("event"))

    return jax.shard_map(shards, mesh=mesh, in_specs=in_specs, out_specs=out_specs, check_vma=False)
```

```python
import math

import jax
import jax.numpy as jnp
import numpy as np
from jax import lax
from jax.experimental import pallas as pl
from jax.experimental.pallas import tpu as pltpu
from jax.sharding import PartitionSpec as P


TIME_STEP = 0.05
EPSILON = 1e-06
F32 = jnp.float32
BF16 = jnp.bfloat16
SAMPLES = 24576


def gll_tables():
    root = math.sqrt(3.0 / 7.0)
    points = np.array([-1.0, -root, 0.0, root, 1.0])
    weights = np.array([0.1, 49.0 / 90.0, 32.0 / 45.0, 49.0 / 90.0, 0.1])
    legendre = (35.0 * points**4 - 30.0 * points**2 + 3.0) / 8.0
    derivative = np.zeros((5, 5))
    for row in range(5):
        for column in range(5):
            if row != column:
                derivative[row, column] = legendre[row] / (
                    legendre[column] * (points[row] - points[column])
                )
    derivative[0, 0] = -5.0
    derivative[4, 4] = 5.0
    return derivative, weights


DERIVATIVE, WEIGHTS = gll_tables()


def apply_line(matrix, u):
    e0, e1 = u[0] + u[4], u[1] + u[3]
    o0, o1 = u[0] - u[4], u[1] - u[3]
    out = [None] * 5
    for s in (0, 1):
        m = matrix[s]
        plus = float(0.5 * (m[0] - m[4])) * o0 + float(0.5 * (m[1] - m[3])) * o1
        minus = (
            float(0.5 * (m[0] + m[4])) * e0
            + float(0.5 * (m[1] + m[3])) * e1
            + float(m[2]) * u[2]
        )
        out[s] = plus + minus
        out[4 - s] = plus - minus
    out[2] = float(matrix[2][0]) * o0 + float(matrix[2][1]) * o1
    return out


def forward_line(u):
    return apply_line(DERIVATIVE, u)


def backward_line(h):
    return apply_line(DERIVATIVE.T, h)


def iotas():
    sub = lax.broadcasted_iota(jnp.int32, (8, 128), 0)
    lane = lax.broadcasted_iota(jnp.int32, (8, 128), 1)
    return sub, lane


def half_turn(v):
    return pltpu.roll(v, 4, 0)


class Shifts:
    def __init__(self):
        sub, lane = iotas()
        self.low = sub < 4
        self.row_first = (sub % 4) == 0
        self.row_last = (sub % 4) == 3
        self.lane_first = lane == 0
        self.lane_last = lane == 127

    def next_y(self, v):
        return jnp.where(self.row_last, 0.0, pltpu.roll(v, 7, 0))

    def next_z(self, v):
        return jnp.where(self.lane_last, 0.0, pltpu.roll(v, 127, 1))

    def carry_y(self, v):
        return jnp.where(self.row_first, 0.0, pltpu.roll(v, 1, 0))

    def carry_z(self, v):
        return jnp.where(self.lane_first, 0.0, pltpu.roll(v, 1, 1))


def pack_low(sh, halves):
    return [
        jnp.where(sh.low, halves[2 * k], half_turn(halves[2 * k + 1])) for k in range(8)
    ]


def pack_high(sh, halves):
    return [
        jnp.where(sh.low, half_turn(halves[2 * k]), halves[2 * k + 1]) for k in range(8)
    ]


def to_high(ref, base, qr):
    v = ref[base + qr // 2]
    return half_turn(v) if qr % 2 == 0 else v


def extended(sh, field, message, base):
    def get(p, qr):
        if p < 4:
            return field[p * 16 + qr]
        return jnp.where(sh.low, half_turn(field[qr]), to_high(message, base, qr))

    return get


def stored(field):
    def get(p, qr):
        return field[p * 16 + qr]

    return get


def expand(sh, get, blocks):
    for p in range(5):
        for r in range(4):
            for q in range(4):
                v = get(p, q * 4 + r)
                blocks[p * 25 + q * 5 + r] = v
                if r == 0:
                    blocks[p * 25 + q * 5 + 4] = sh.next_z(v)
                if q == 0:
                    far = sh.next_y(v)
                    blocks[p * 25 + 20 + r] = far
                    if r == 0:
                        blocks[p * 25 + 24] = sh.next_z(far)


def line_indices(direction, a, b):
    if direction == 0:
        return [k * 25 + a * 5 + b for k in range(5)]
    if direction == 1:
        return [a * 25 + k * 5 + b for k in range(5)]
    return [a * 25 + b * 5 + k for k in range(5)]


def force(sh, blocks, stiff, scratch, out):
    for q in range(5):
        for r in range(5):
            at = line_indices(0, q, r)
            g = forward_line([blocks[i] for i in at])
            f = backward_line([stiff[i] * g[k] for k, i in enumerate(at)])
            for k, i in enumerate(at):
                scratch[i] = f[k]
    for p in range(5):
        total = {}
        for q in range(5):
            at = line_indices(2, p, q)
            g = forward_line([blocks[i] for i in at])
            f = backward_line([stiff[i] * g[k] for k, i in enumerate(at)])
            for k, i in enumerate(at):
                total[i] = scratch[i] + f[k]
        for r in range(5):
            at = line_indices(1, p, r)
            g = forward_line([blocks[i] for i in at])
            f = backward_line([stiff[i] * g[k] for k, i in enumerate(at)])
            for k, i in enumerate(at):
                total[i] = total[i] + f[k]
        for qr, v in enumerate(assemble(sh, [total[p * 25 + n] for n in range(25)])):
            out[p * 16 + qr] = v


def assemble(sh, face):
    rows = {}
    for q in range(5):
        rows[q, 0] = face[q * 5] + sh.carry_z(face[q * 5 + 4])
        for r in range(1, 4):
            rows[q, r] = face[q * 5 + r]
    nodes = []
    for q in range(4):
        for r in range(4):
            nodes.append(rows[0, r] + sh.carry_y(rows[4, r]) if q == 0 else rows[q, r])
    return nodes


def products(first, second, acc, initial):
    for direction in range(3):
        for a in range(5):
            for b in range(5):
                at = line_indices(direction, a, b)
                g = forward_line([first[i] for i in at])
                h = forward_line([second[i] for i in at])
                for k, i in enumerate(at):
                    if initial and direction == 0:
                        acc[i] = g[k] * h[k]
                    else:
                        acc[i] = acc[i] + g[k] * h[k]


def assembled(sh, forces, incoming, base):
    def total(p, qr):
        f = forces[p * 16 + qr]
        if p == 0:
            return f + jnp.where(
                sh.low, incoming.from_left(base, qr), half_turn(forces[64 + qr])
            )
        if p == 4:
            return f + jnp.where(
                sh.low, half_turn(forces[qr]), incoming.from_right(base, qr)
            )
        return f

    return total


def put_messages(sh, odd, forces, far, near, base):
    to_left = pack_low(sh, [forces[qr] for qr in range(16)])
    to_right = pack_high(sh, [forces[64 + qr] for qr in range(16)])
    for k in range(8):
        far[base + k] = jnp.where(odd, to_right[k], to_left[k])
        near[base + k] = jnp.where(odd, to_left[k], to_right[k])


class Incoming:
    def __init__(self, odd, far, near):
        self.odd, self.far, self.near = odd, far, near

    def from_left(self, base, qr):
        at = base + qr // 2
        v = jnp.where(self.odd, self.near[at], self.far[at])
        return v if qr % 2 == 0 else half_turn(v)

    def from_right(self, base, qr):
        at = base + qr // 2
        v = jnp.where(self.odd, self.far[at], self.near[at])
        return half_turn(v) if qr % 2 == 0 else v


def is_odd(slab_ref):
    return slab_ref[0] % 2 == 1


def split3(x):
    hi = x.astype(BF16)
    rest = x - hi.astype(F32)
    mid = rest.astype(BF16)
    lo = (rest - mid.astype(F32)).astype(BF16)
    return hi, mid, lo


def selection(swap):
    z = lax.broadcasted_iota(jnp.int32, (256, 256), 0)
    c = lax.broadcasted_iota(jnp.int32, (256, 256), 1)
    r = c // 64
    if swap:
        r = r + 1 - 2 * (r % 2)
    return jnp.where(z == 4 * (c % 64) + r, 1.0, 0.0).astype(BF16)


def to_local(x_ref, near, far, rows, emit):
    x = jnp.concatenate([x_ref[4 * i + p] for p in range(4) for i in range(2)], axis=0)
    first = second = None
    for part in split3(x):
        a = jnp.dot(part[:, :256], near, preferred_element_type=F32)
        b = jnp.dot(part[:, 256:], far, preferred_element_type=F32)
        first = a if first is None else first + a
        second = b if second is None else second + b
    lower = lax.broadcasted_iota(jnp.int32, (128, 128), 1) < 64
    for half in range(2):
        a = first[:, 128 * half : 128 * half + 128]
        b = second[:, 128 * half : 128 * half + 128]
        rows[2 * half] = jnp.where(lower, a, b)
        rows[2 * half + 1] = pltpu.roll(jnp.where(lower, b, a), 64, 1)
    for p in range(4):
        for q in range(4):
            for r in range(4):
                emit(p, q * 4 + r, rows[r, pl.ds(32 * p + q, 8, stride=4), :])


def facts_kernel(receivers_ref, observed_ref, out):
    out[0:1, :] = receivers_ref[...].astype(F32)
    energy = jnp.zeros((1, 128), F32)
    for step in range(3):
        values = observed_ref[step]
        energy = energy + values * values
        if step < 2:
            out[step + 1 : step + 2, :] = values
    out[3:4, :] = energy


def first_kernel(states_ref, facts_ref, u_out, lam_out, message, rows):
    sh = Shifts()
    near, far = selection(False), selection(True)
    for which, target in enumerate((u_out, lam_out)):

        def emit(p, qr, v, target=target):
            target[p * 16 + qr] = v

        to_local(states_ref.at[which], near, far, rows, emit)
        for k, v in enumerate(pack_low(sh, [target[qr] for qr in range(16)])):
            message[8 * which + k] = v
    message[16] = jnp.zeros((8, 128), F32)
    message[16, 0:4, :] = facts_ref[...]


def receiver_rows(receivers):
    x, yz = receivers // 8192, receivers % 8192
    y, z = yz // 512, yz % 512
    i, p, j, q, r = x // 4, x % 4, y // 4, y % 4, z % 4
    return ((p * 4 + q) * 4 + r) * 8 + i * 4 + j, z // 4


def one_hots(receivers):
    row, lane = receiver_rows(receivers)
    row_hot = lax.broadcasted_iota(jnp.int32, (512, 128), 0) == row
    lane_hot = lax.broadcasted_iota(jnp.int32, (128, 128), 0) == lane
    return row_hot, lane_hot


def second_kernel(
    slab_ref, fields_ref, modulus_ref, prev_out, next_out, scale_out, stiff_out, message, rows
):
    sh = Shifts()
    near, far = selection(False), selection(True)
    for which, target in enumerate((prev_out, next_out)):

        def emit(p, qr, v, target=target):
            target[p * 16 + qr] = v

        to_local(fields_ref.at[which], near, far, rows, emit)
    line = (0.2, 49.0 / 90.0, 32.0 / 45.0, 49.0 / 90.0)
    first_x = jnp.logical_and(sh.low, slab_ref[0] == 0)

    def emit_scale(p, qr, v):
        q, r = qr // 4, qr % 4
        mass = v * (jnp.where(first_x, 0.1, 0.2).astype(F32) if p == 0 else line[p])
        mass = mass * (jnp.where(sh.row_first, 0.1, 0.2).astype(F32) if q == 0 else line[q])
        mass = mass * (jnp.where(sh.lane_first, 0.1, 0.2).astype(F32) if r == 0 else line[r])
        scale_out[p * 16 + qr] = (TIME_STEP * TIME_STEP) / mass

    to_local(fields_ref.at[2], near, far, rows, emit_scale)
    for p in range(5):
        for q in range(5):
            for r in range(5):
                weight = float(WEIGHTS[p] * WEIGHTS[q] * WEIGHTS[r])
                block = jnp.concatenate(
                    [modulus_ref[p, 0, q, r], modulus_ref[p, 1, q, r]], axis=0
                )
                stiff_out[p * 25 + q * 5 + r] = weight * block
    for which, field in enumerate((prev_out, next_out, scale_out)):
        for k, v in enumerate(pack_low(sh, [field[qr] for qr in range(16)])):
            message[8 * which + k] = v


def count_kernel(receivers_ref, observed_ref, message, counts_out, far_out):
    contract = (((1,), (1,)), ((), ()))

    def counted(receivers, observed, nodes):
        row, lane = receiver_rows(receivers)
        row_hot = lax.broadcasted_iota(jnp.int32, (nodes, 128), 0) == row
        row_hot = jnp.where(row_hot, 1.0, 0.0).astype(BF16)
        lane_hot = lax.broadcasted_iota(jnp.int32, (128, 128), 0) == lane
        ones = jnp.where(lane_hot, 1.0, 0.0).astype(BF16)
        totals = [lax.dot_general(row_hot, ones, contract, preferred_element_type=F32)]
        for values in observed:
            total = None
            for part in split3(jnp.where(lane_hot, values, 0.0)):
                t = lax.dot_general(row_hot, part, contract, preferred_element_type=F32)
                total = t if total is None else total + t
            totals.append(total)
        return totals

    own = counted(receivers_ref[...], [observed_ref[0], observed_ref[1]], 512)
    for which, total in enumerate(own):
        for n in range(64):
            counts_out[which * 64 + n] = total[8 * n : 8 * n + 8]
    theirs = counted(
        message[16, 0:1, :].astype(jnp.int32), [message[16, 1:2, :], message[16, 2:3, :]], 128
    )
    for which, total in enumerate(theirs):
        for n in range(16):
            far_out[which * 16 + n] = half_turn(total[8 * n : 8 * n + 8])


def without_far(sh, field):
    def get(p, qr):
        if p < 4:
            return field[p * 16 + qr]
        return jnp.where(sh.low, half_turn(field[qr]), 0.0)

    return get


def force_kernel(u_ref, lam_ref, stiff, u_force, lam_force, blocks, scratch):
    sh = Shifts()
    for field, out in ((u_ref, u_force), (lam_ref, lam_force)):
        expand(sh, without_far(sh, field), blocks)
        force(sh, blocks, stiff, scratch, out)


def far_plane_kernel(
    slab_ref, message, stiff, u_in, lam_in, u_force, lam_force, far, near, column
):
    sh = Shifts()
    odd = is_odd(slab_ref)
    for n in range(25):
        f = backward_line([float(DERIVATIVE[k, 4]) * stiff[k * 25 + n] for k in range(5)])
        for k in range(5):
            column[k * 25 + n] = f[k]
    for which, (source, out) in enumerate(((u_in, u_force), (lam_in, lam_force))):
        face = [None] * 25
        for q in range(4):
            for r in range(4):
                v = jnp.where(sh.low, 0.0, to_high(message, 8 * which, q * 4 + r))
                face[q * 5 + r] = v
                if r == 0:
                    face[q * 5 + 4] = sh.next_z(v)
                if q == 0:
                    face[20 + r] = sh.next_y(v)
                    if r == 0:
                        face[24] = sh.next_z(face[20])
        for p in range(5):
            added = [column[p * 25 + n] * face[n] for n in range(25)]
            if p == 4:
                for a in range(5):
                    for at in ([a * 5 + k for k in range(5)], [k * 5 + a for k in range(5)]):
                        g = forward_line([face[n] for n in at])
                        f = backward_line([stiff[100 + n] * g[k] for k, n in enumerate(at)])
                        for k, n in enumerate(at):
                            added[n] = added[n] + f[k]
            for qr, v in enumerate(assemble(sh, added)):
                out[p * 16 + qr] = source[p * 16 + qr] + v
        put_messages(sh, odd, out, far, near, 8 * which)


def step_one_kernel(
    slab_ref,
    u_ref,
    lam_ref,
    prev_ref,
    next_ref,
    scale_ref,
    stiff,
    message0,
    message1,
    u_force,
    lam_force,
    far_in,
    near_in,
    u1_out,
    lam1_out,
    scale_out,
    u1_force,
    lam1_force,
    far,
    near,
    blocks,
    scratch,
):
    sh = Shifts()
    odd = is_odd(slab_ref)
    incoming = Incoming(odd, far_in, near_in)
    u0, lam2 = extended(sh, u_ref, message0, 0), extended(sh, lam_ref, message0, 8)
    before, after = extended(sh, prev_ref, message1, 0), extended(sh, next_ref, message1, 8)
    scale = extended(sh, scale_ref, message1, 16)
    u_total = assembled(sh, u_force, incoming, 0)
    lam_total = assembled(sh, lam_force, incoming, 8)
    for p in range(5):
        for qr in range(16):
            s = scale(p, qr)
            scale_out[p * 16 + qr] = s
            u1_out[p * 16 + qr] = 2.0 * u0(p, qr) - before(p, qr) - s * u_total(p, qr)
            lam1_out[p * 16 + qr] = 2.0 * lam2(p, qr) - after(p, qr) - s * lam_total(p, qr)
    for which, (field, out) in enumerate(((u1_out, u1_force), (lam1_out, lam1_force))):
        expand(sh, stored(field), blocks)
        force(sh, blocks, stiff, scratch, out)
        put_messages(sh, odd, out, far, near, 8 * which)


def mean_square(energy):
    total = jnp.sum(energy[3:4], axis=1, keepdims=True)
    return total / SAMPLES + EPSILON


def step_two_kernel(
    slab_ref,
    u_ref,
    lam_ref,
    message0,
    u1_ref,
    lam1_ref,
    scale,
    counts,
    far_counts,
    stiff,
    u1_force,
    lam1_force,
    far_in,
    near_in,
    u2_out,
    driven1_out,
    lam0_out,
    source_out,
    driven1_force,
    far,
    near,
    blocks,
    scratch,
):
    u2_force = u2_out.at[pl.ds(80, 80)]
    sh = Shifts()
    odd = is_odd(slab_ref)
    incoming = Incoming(odd, far_in, near_in)
    u0, lam2 = extended(sh, u_ref, message0, 0), extended(sh, lam_ref, message0, 8)

    def nodal(which):
        def get(p, qr):
            if p < 4:
                return counts[64 * which + p * 16 + qr]
            return jnp.where(
                sh.low, half_turn(counts[64 * which + qr]), far_counts[16 * which + qr]
            )

        return get

    count, seen = nodal(0), (nodal(1), nodal(2))
    u_total = assembled(sh, u1_force, incoming, 0)
    lam_total = assembled(sh, lam1_force, incoming, 8)
    for p in range(5):
        for qr in range(16):
            at = p * 16 + qr
            s, u1, c = scale[at], u1_ref[at], count(p, qr)
            u2 = 2.0 * u1 - u0(p, qr) - s * u_total(p, qr)
            u2_out[at] = u2
            driven1_out[at] = s * (c * u2 - seen[1](p, qr))
            source_out[at] = s * (c * u1 - seen[0](p, qr))
            lam0_out[at] = 2.0 * lam1_ref[at] - lam2(p, qr) - s * lam_total(p, qr)
    pairs = ((driven1_out, driven1_force), (u2_out, u2_force))
    for which, (field, out) in enumerate(pairs):
        expand(sh, stored(field), blocks)
        force(sh, blocks, stiff, scratch, out)
        put_messages(sh, odd, out, far, near, 8 * which)


def middle_kernel(
    u_ref,
    lam_ref,
    message0,
    u1_ref,
    lam1_ref,
    u2_ref,
    driven1_ref,
    lam0_ref,
    scale,
    acc,
    driven_acc,
    u3_out,
    first,
    second,
):
    sh = Shifts()
    for at in range(64):
        f = u2_ref[80 + at]
        if at < 16:
            f = f + jnp.where(sh.low, 0.0, half_turn(u2_ref[144 + at]))
        u3_out[at] = 2.0 * u2_ref[at] - u1_ref[at] - scale[at] * f
    expand(sh, stored(u1_ref), first)
    expand(sh, stored(driven1_ref), second)
    products(first, second, driven_acc, True)
    expand(sh, stored(lam1_ref), second)
    products(first, second, acc, True)
    expand(sh, stored(u2_ref), first)
    expand(sh, extended(sh, lam_ref, message0, 8), second)
    products(first, second, acc, False)
    expand(sh, extended(sh, u_ref, message0, 0), first)
    expand(sh, stored(lam0_ref), second)
    products(first, second, acc, False)


def last_kernel(
    slab_ref,
    event_ref,
    energy_ref,
    u_ref,
    message0,
    driven1_ref,
    scale,
    source,
    driven1_force,
    far_in,
    near_in,
    acc_ref,
    driven_acc_ref,
    out0,
    out1,
    out2,
    out3,
    driven0,
    first,
    second,
    acc,
    flat,
):
    sh = Shifts()
    total = assembled(sh, driven1_force, Incoming(is_odd(slab_ref), far_in, near_in), 0)
    for p in range(5):
        for qr in range(16):
            at = p * 16 + qr
            driven0[at] = 2.0 * driven1_ref[at] - scale[at] * total(p, qr) + source[at]
    expand(sh, extended(sh, u_ref, message0, 0), first)
    expand(sh, stored(driven0), second)
    for i in range(125):
        acc[i] = driven_acc_ref[i]
    products(first, second, acc, False)
    inverse = jnp.broadcast_to(1.0 / mean_square(energy_ref[...]), (8, 128))
    for p in range(5):
        for q in range(5):
            for r in range(5):
                at = p * 25 + q * 5 + r
                weight = float(-WEIGHTS[p] * WEIGHTS[q] * WEIGHTS[r])
                v = weight * (acc_ref[at] + inverse * acc[at])
                for i in range(2):
                    row = 4 * ((2 * p + i) * 25 + q * 5 + r)
                    flat[row : row + 4, :] = v[4 * i : 4 * i + 4]
    event = event_ref[0]
    for k, out in enumerate((out0, out1, out2, out3)):
        out[...] = flat[pl.ds(jnp.bitwise_xor(event, k), 250, stride=4), :]


def misfit_kernel(
    slab_ref,
    receivers_ref,
    observed_ref,
    u1_ref,
    u2_ref,
    u3_ref,
    scale,
    far_in,
    near_in,
    out,
    u3,
):
    sh = Shifts()
    incoming = Incoming(is_odd(slab_ref), far_in, near_in)
    for at in range(64):
        v = u3_ref[at]
        if at < 16:
            v = v - scale[at] * jnp.where(sh.low, incoming.from_left(8, at), 0.0)
        u3[at] = v
    row_hot, lane_hot = one_hots(receivers_ref[...])
    row_hot = jnp.where(row_hot, 1.0, 0.0).astype(BF16)
    squares = jnp.zeros((1, 128), F32)
    for step, field in enumerate((u1_ref, u2_ref, u3)):
        values = field[pl.ds(0, 64)].reshape(512, 128)
        picked = None
        for part in split3(values):
            t = lax.dot_general(
                part, row_hot, (((0,), (0,)), ((), ())), preferred_element_type=F32
            )
            picked = t if picked is None else picked + t
        syn = jnp.sum(jnp.where(lane_hot, picked, 0.0), axis=0, keepdims=True)
        residual = syn - observed_ref[step]
        squares = squares + residual * residual
    out[...] = jnp.broadcast_to(jnp.sum(squares, axis=1, keepdims=True), (1, 128))


def sum_kernel(a, b, c, d, misfit, total_out, message):
    total = a[...] + b[...] + c[...] + d[...]
    total_out[...] = total
    largest = jnp.max(jnp.max(jnp.abs(total), axis=0, keepdims=True), axis=1, keepdims=True)
    first_half = lax.broadcasted_iota(jnp.int32, (1, 128), 1) < 64
    message[...] = jnp.where(first_half, jnp.broadcast_to(largest, (1, 128)), misfit[...])


def divide_kernel(event_ref, total, gathered, energy_ref, out, misfit_out):
    rows = gathered[...]
    first_half = lax.broadcasted_iota(jnp.int32, (1, 128), 1) < 64
    top = jnp.where(first_half, jnp.max(rows, axis=0, keepdims=True), 0.0)
    largest = jnp.max(top, axis=1, keepdims=True)
    spaces = gathered.shape[0] // 4
    mine = gathered[pl.ds(pl.multiple_of(event_ref[0] * spaces, spaces), spaces), :]
    squares = jnp.where(first_half, 0.0, jnp.sum(mine, axis=0, keepdims=True))
    squares = jnp.max(squares, axis=1, keepdims=True)
    misfit_out[...] = jnp.broadcast_to(
        0.5 * squares / (SAMPLES * mean_square(energy_ref[...])), (1, 128)
    )
    out[...] = (total[...] / (largest + EPSILON)).reshape(250, 1, 128)


COST = 16 << 20
VMEM_GRANT = 8 << 20
VMEM_SPEC = pl.BlockSpec(memory_space=pltpu.VMEM)
SMEM_SPEC = pl.BlockSpec(memory_space=pltpu.SMEM)


def call(kernel, args, outs, scratch=(), scalars=0):
    return pl.pallas_call(
        kernel,
        out_shape=[jax.ShapeDtypeStruct(shape, F32) for shape in outs],
        in_specs=[SMEM_SPEC] * scalars + [VMEM_SPEC] * (len(args) - scalars),
        out_specs=[VMEM_SPEC] * len(outs),
        scratch_shapes=[pltpu.VMEM(shape, F32) for shape in scratch],
        cost_estimate=pl.CostEstimate(flops=0, bytes_accessed=COST, transcendentals=0),
        compiler_params=pltpu.CompilerParams(vmem_limit_bytes=VMEM_GRANT),
    )(*args)


def vectors(count):
    return (count, 8, 128)


def send(array, axis, pairs):
    return lax.ppermute(array, axis, pairs)


def to_left(array):
    devices = lax.axis_size("space")
    return send(array, "space", [(i, i - 1) for i in range(1, devices)])


def exchange(far, near):
    devices = lax.axis_size("space")
    far_pairs = [(i, i + 1 if i % 2 else i - 1) for i in range(1, devices - 1)]
    near_pairs = [(i, i - 1 if i % 2 else i + 1) for i in range(devices)]
    return (send(far, "space", far_pairs), send(near, "space", near_pairs))


def across(array, stride):
    devices = lax.axis_size("space")
    return array + send(array, "space", [(i, i ^ stride) for i in range(devices)])


def shards(state_now, state_prev, adjoint_now, adjoint_next, modulus, density, receivers, observed):
    slab = lax.axis_index("space").astype(jnp.int32).reshape(1)
    event = lax.axis_index("event").astype(jnp.int32).reshape(1)
    receivers = receivers.reshape(1, 128)
    observed = jnp.transpose(observed, (1, 0, 2))
    modulus = jnp.transpose(modulus, (0, 1, 2, 4, 3, 5))

    (facts,) = call(facts_kernel, (receivers, observed), [(4, 128)])
    energy = across(facts, 1)

    u0, lam2, planes = call(
        first_kernel,
        (jnp.stack([state_now[0], adjoint_now[0]]), facts),
        [vectors(64), vectors(64), vectors(17)],
        [(4, 128, 128)],
    )
    message0 = to_left(planes)
    energy = across(energy, 16)
    before, after, scale, stiff, planes = call(
        second_kernel,
        (slab, jnp.stack([state_prev[0], adjoint_next[0], density]), modulus),
        [vectors(64), vectors(64), vectors(64), vectors(125), vectors(24)],
        [(4, 128, 128)],
        scalars=1,
    )
    u_force, lam_force = call(
        force_kernel,
        (u0, lam2, stiff),
        [vectors(80), vectors(80)],
        [vectors(125), vectors(125)],
    )
    message1 = to_left(planes)
    energy = across(energy, 2)
    counts, far_counts = call(
        count_kernel, (receivers, observed, message0), [vectors(192), vectors(48)]
    )
    u_force, lam_force, far, near = call(
        far_plane_kernel,
        (slab, message0, stiff, u_force, lam_force),
        [vectors(80), vectors(80), vectors(16), vectors(16)],
        [vectors(125)],
        scalars=1,
    )
    energy = across(energy, 32)
    far, near = exchange(far, near)
    u1, lam1, scale, u1_force, lam1_force, far, near = call(
        step_one_kernel,
        (
            slab,
            u0,
            lam2,
            before,
            after,
            scale,
            stiff,
            message0,
            message1,
            u_force,
            lam_force,
            far,
            near,
        ),
        [vectors(80)] * 5 + [vectors(16)] * 2,
        [vectors(125), vectors(125)],
        scalars=1,
    )
    energy = across(energy, 4)
    energy = across(energy, 8)
    far, near = exchange(far, near)
    u2, driven1, lam0, source, driven1_force, far, near = call(
        step_two_kernel,
        (
            slab,
            u0,
            lam2,
            message0,
            u1,
            lam1,
            scale,
            counts,
            far_counts,
            stiff,
            u1_force,
            lam1_force,
            far,
            near,
        ),
        [vectors(160)] + [vectors(80)] * 4 + [vectors(16)] * 2,
        [vectors(125), vectors(125)],
        scalars=1,
    )
    far, near = exchange(far, near)
    acc, driven_acc, u3 = call(
        middle_kernel,
        (u0, lam2, message0, u1, lam1, u2, driven1, lam0, scale),
        [vectors(125), vectors(125), vectors(64)],
        [vectors(125), vectors(125)],
    )
    pieces = call(
        last_kernel,
        (
            slab,
            event,
            energy,
            u0,
            message0,
            driven1,
            scale,
            source,
            driven1_force,
            far,
            near,
            acc,
            driven_acc,
        ),
        [(250, 128)] * 4,
        [vectors(80), vectors(125), vectors(125), vectors(125), (1000, 128)],
        scalars=2,
    )
    events = lax.axis_size("event")
    others = [send(pieces[k], "event", [(i, i ^ k) for i in range(events)]) for k in (1, 2, 3)]
    (squares,) = call(
        misfit_kernel,
        (slab, receivers, observed, u1, u2, u3, scale, far, near),
        [(1, 128)],
        [vectors(64)],
        scalars=1,
    )
    total, message = call(
        sum_kernel, (pieces[0], *others, squares), [(250, 128), (1, 128)]
    )
    everyone = ("event", "space")
    devices = lax.axis_size("event") * lax.axis_size("space")
    gathered = lax.all_to_all(
        jnp.broadcast_to(message[None], (devices, 1, 128)), everyone, 0, 0
    )
    kernel, misfit = call(
        divide_kernel,
        (event, total, gathered.reshape(devices, 128), energy),
        [(250, 1, 128), (1, 128)],
        scalars=1,
    )
    kernel = jnp.transpose(kernel.reshape(5, 2, 5, 5, 1, 128), (0, 1, 2, 4, 3, 5))
    return (kernel, misfit[0, :1])


def solution(mesh):
    in_specs = (
        P("event", "space", None, None),
        P("event", "space", None, None),
        P("event", "space", None, None),
        P("event", "space", None, None),
        P(None, "space", None, None, None, None),
        P("space", None, None),
        P("space"),
        P("event", None, "space"),
    )
    out_specs = (P(None, "space", None, "event", None, None), P("event"))

    return jax.shard_map(shards, mesh=mesh, in_specs=in_specs, out_specs=out_specs, check_vma=False)
```

```python
import math

import jax
import jax.numpy as jnp
import numpy as np
from jax import lax
from jax.experimental import pallas as pl
from jax.experimental.pallas import tpu as pltpu
from jax.sharding import PartitionSpec as P


TIME_STEP = 0.05
EPSILON = 1e-06
F32 = jnp.float32
BF16 = jnp.bfloat16
SAMPLES = 24576


def gll_tables():
    root = math.sqrt(3.0 / 7.0)
    points = np.array([-1.0, -root, 0.0, root, 1.0])
    weights = np.array([0.1, 49.0 / 90.0, 32.0 / 45.0, 49.0 / 90.0, 0.1])
    legendre = (35.0 * points**4 - 30.0 * points**2 + 3.0) / 8.0
    derivative = np.zeros((5, 5))
    for row in range(5):
        for column in range(5):
            if row != column:
                derivative[row, column] = legendre[row] / (
                    legendre[column] * (points[row] - points[column])
                )
    derivative[0, 0] = -5.0
    derivative[4, 4] = 5.0
    return derivative, weights


DERIVATIVE, WEIGHTS = gll_tables()


def apply_line(matrix, u):
    e0, e1 = u[0] + u[4], u[1] + u[3]
    o0, o1 = u[0] - u[4], u[1] - u[3]
    out = [None] * 5
    for s in (0, 1):
        m = matrix[s]
        plus = float(0.5 * (m[0] - m[4])) * o0 + float(0.5 * (m[1] - m[3])) * o1
        minus = (
            float(0.5 * (m[0] + m[4])) * e0
            + float(0.5 * (m[1] + m[3])) * e1
            + float(m[2]) * u[2]
        )
        out[s] = plus + minus
        out[4 - s] = plus - minus
    out[2] = float(matrix[2][0]) * o0 + float(matrix[2][1]) * o1
    return out


def forward_line(u):
    return apply_line(DERIVATIVE, u)


def backward_line(h):
    return apply_line(DERIVATIVE.T, h)


def iotas():
    sub = lax.broadcasted_iota(jnp.int32, (8, 128), 0)
    lane = lax.broadcasted_iota(jnp.int32, (8, 128), 1)
    return sub, lane


def half_turn(v):
    return pltpu.roll(v, 4, 0)


class Shifts:
    def __init__(self):
        sub, lane = iotas()
        self.low = sub < 4
        self.row_first = (sub % 4) == 0
        self.row_last = (sub % 4) == 3
        self.lane_first = lane == 0
        self.lane_last = lane == 127

    def next_y(self, v):
        return jnp.where(self.row_last, 0.0, pltpu.roll(v, 7, 0))

    def next_z(self, v):
        return jnp.where(self.lane_last, 0.0, pltpu.roll(v, 127, 1))

    def carry_y(self, v):
        return jnp.where(self.row_first, 0.0, pltpu.roll(v, 1, 0))

    def carry_z(self, v):
        return jnp.where(self.lane_first, 0.0, pltpu.roll(v, 1, 1))


def pack_low(sh, halves):
    return [
        jnp.where(sh.low, halves[2 * k], half_turn(halves[2 * k + 1])) for k in range(8)
    ]


def pack_high(sh, halves):
    return [
        jnp.where(sh.low, half_turn(halves[2 * k]), halves[2 * k + 1]) for k in range(8)
    ]


def to_high(ref, base, qr):
    v = ref[base + qr // 2]
    return half_turn(v) if qr % 2 == 0 else v


def extended(sh, field, message, base):
    def get(p, qr):
        if p < 4:
            return field[p * 16 + qr]
        return jnp.where(sh.low, half_turn(field[qr]), to_high(message, base, qr))

    return get


def stored(field):
    def get(p, qr):
        return field[p * 16 + qr]

    return get


def expand(sh, get, blocks):
    for p in range(5):
        for r in range(4):
            for q in range(4):
                v = get(p, q * 4 + r)
                blocks[p * 25 + q * 5 + r] = v
                if r == 0:
                    blocks[p * 25 + q * 5 + 4] = sh.next_z(v)
                if q == 0:
                    far = sh.next_y(v)
                    blocks[p * 25 + 20 + r] = far
                    if r == 0:
                        blocks[p * 25 + 24] = sh.next_z(far)


def line_indices(direction, a, b):
    if direction == 0:
        return [k * 25 + a * 5 + b for k in range(5)]
    if direction == 1:
        return [a * 25 + k * 5 + b for k in range(5)]
    return [a * 25 + b * 5 + k for k in range(5)]


def force(sh, blocks, stiff, scratch, out):
    for q in range(5):
        for r in range(5):
            at = line_indices(0, q, r)
            g = forward_line([blocks[i] for i in at])
            f = backward_line([stiff[i] * g[k] for k, i in enumerate(at)])
            for k, i in enumerate(at):
                scratch[i] = f[k]
    for p in range(5):
        total = {}
        for q in range(5):
            at = line_indices(2, p, q)
            g = forward_line([blocks[i] for i in at])
            f = backward_line([stiff[i] * g[k] for k, i in enumerate(at)])
            for k, i in enumerate(at):
                total[i] = scratch[i] + f[k]
        for r in range(5):
            at = line_indices(1, p, r)
            g = forward_line([blocks[i] for i in at])
            f = backward_line([stiff[i] * g[k] for k, i in enumerate(at)])
            for k, i in enumerate(at):
                total[i] = total[i] + f[k]
        for qr, v in enumerate(assemble(sh, [total[p * 25 + n] for n in range(25)])):
            out[p * 16 + qr] = v


def assemble(sh, face):
    rows = {}
    for q in range(5):
        rows[q, 0] = face[q * 5] + sh.carry_z(face[q * 5 + 4])
        for r in range(1, 4):
            rows[q, r] = face[q * 5 + r]
    nodes = []
    for q in range(4):
        for r in range(4):
            nodes.append(rows[0, r] + sh.carry_y(rows[4, r]) if q == 0 else rows[q, r])
    return nodes


def products(first, second, acc, initial):
    for direction in range(3):
        for a in range(5):
            for b in range(5):
                at = line_indices(direction, a, b)
                g = forward_line([first[i] for i in at])
                h = forward_line([second[i] for i in at])
                for k, i in enumerate(at):
                    if initial and direction == 0:
                        acc[i] = g[k] * h[k]
                    else:
                        acc[i] = acc[i] + g[k] * h[k]


def assembled(sh, forces, incoming, base):
    def total(p, qr):
        f = forces[p * 16 + qr]
        if p == 0:
            return f + jnp.where(
                sh.low, incoming.from_left(base, qr), half_turn(forces[64 + qr])
            )
        if p == 4:
            return f + jnp.where(
                sh.low, half_turn(forces[qr]), incoming.from_right(base, qr)
            )
        return f

    return total


def put_messages(sh, odd, forces, far, near, base):
    to_left = pack_low(sh, [forces[qr] for qr in range(16)])
    to_right = pack_high(sh, [forces[64 + qr] for qr in range(16)])
    for k in range(8):
        far[base + k] = jnp.where(odd, to_right[k], to_left[k])
        near[base + k] = jnp.where(odd, to_left[k], to_right[k])


class Incoming:
    def __init__(self, odd, far, near):
        self.odd, self.far, self.near = odd, far, near

    def from_left(self, base, qr):
        at = base + qr // 2
        v = jnp.where(self.odd, self.near[at], self.far[at])
        return v if qr % 2 == 0 else half_turn(v)

    def from_right(self, base, qr):
        at = base + qr // 2
        v = jnp.where(self.odd, self.far[at], self.near[at])
        return half_turn(v) if qr % 2 == 0 else v


def is_odd(slab_ref):
    return slab_ref[0] % 2 == 1


def split3(x):
    hi = x.astype(BF16)
    rest = x - hi.astype(F32)
    mid = rest.astype(BF16)
    lo = (rest - mid.astype(F32)).astype(BF16)
    return hi, mid, lo


def selection(swap):
    z = lax.broadcasted_iota(jnp.int32, (256, 256), 0)
    c = lax.broadcasted_iota(jnp.int32, (256, 256), 1)
    r = c // 64
    if swap:
        r = r + 1 - 2 * (r % 2)
    return jnp.where(z == 4 * (c % 64) + r, 1.0, 0.0).astype(BF16)


def to_local(x_ref, near, far, rows, emit):
    x = jnp.concatenate([x_ref[4 * i + p] for p in range(4) for i in range(2)], axis=0)
    first = second = None
    for part in split3(x):
        a = jnp.dot(part[:, :256], near, preferred_element_type=F32)
        b = jnp.dot(part[:, 256:], far, preferred_element_type=F32)
        first = a if first is None else first + a
        second = b if second is None else second + b
    lower = lax.broadcasted_iota(jnp.int32, (128, 128), 1) < 64
    for half in range(2):
        a = first[:, 128 * half : 128 * half + 128]
        b = second[:, 128 * half : 128 * half + 128]
        rows[2 * half] = jnp.where(lower, a, b)
        rows[2 * half + 1] = pltpu.roll(jnp.where(lower, b, a), 64, 1)
    for p in range(4):
        for q in range(4):
            for r in range(4):
                emit(p, q * 4 + r, rows[r, pl.ds(32 * p + q, 8, stride=4), :])


def facts_kernel(receivers_ref, observed_ref, out):
    out[0:1, :] = receivers_ref[...].astype(F32)
    energy = jnp.zeros((1, 128), F32)
    for step in range(3):
        values = observed_ref[step]
        energy = energy + values * values
        if step < 2:
            out[step + 1 : step + 2, :] = values
    out[3:4, :] = energy


def first_kernel(states_ref, facts_ref, u_out, lam_out, message, rows):
    sh = Shifts()
    near, far = selection(False), selection(True)
    for which, target in enumerate((u_out, lam_out)):

        def emit(p, qr, v, target=target):
            target[p * 16 + qr] = v

        to_local(states_ref.at[which], near, far, rows, emit)
        for k, v in enumerate(pack_low(sh, [target[qr] for qr in range(16)])):
            message[8 * which + k] = v
    message[16] = jnp.zeros((8, 128), F32)
    message[16, 0:4, :] = facts_ref[...]


def receiver_rows(receivers):
    x, yz = receivers // 8192, receivers % 8192
    y, z = yz // 512, yz % 512
    i, p, j, q, r = x // 4, x % 4, y // 4, y % 4, z % 4
    return ((p * 4 + q) * 4 + r) * 8 + i * 4 + j, z // 4


def one_hots(receivers):
    row, lane = receiver_rows(receivers)
    row_hot = lax.broadcasted_iota(jnp.int32, (512, 128), 0) == row
    lane_hot = lax.broadcasted_iota(jnp.int32, (128, 128), 0) == lane
    return row_hot, lane_hot


def second_kernel(
    slab_ref, fields_ref, modulus_ref, prev_out, next_out, scale_out, stiff_out, message, rows
):
    sh = Shifts()
    near, far = selection(False), selection(True)
    for which, target in enumerate((prev_out, next_out)):

        def emit(p, qr, v, target=target):
            target[p * 16 + qr] = v

        to_local(fields_ref.at[which], near, far, rows, emit)
    line = (0.2, 49.0 / 90.0, 32.0 / 45.0, 49.0 / 90.0)
    first_x = jnp.logical_and(sh.low, slab_ref[0] == 0)

    def emit_scale(p, qr, v):
        q, r = qr // 4, qr % 4
        mass = v * (jnp.where(first_x, 0.1, 0.2).astype(F32) if p == 0 else line[p])
        mass = mass * (jnp.where(sh.row_first, 0.1, 0.2).astype(F32) if q == 0 else line[q])
        mass = mass * (jnp.where(sh.lane_first, 0.1, 0.2).astype(F32) if r == 0 else line[r])
        scale_out[p * 16 + qr] = (TIME_STEP * TIME_STEP) / mass

    to_local(fields_ref.at[2], near, far, rows, emit_scale)
    for p in range(5):
        for q in range(5):
            for r in range(5):
                weight = float(WEIGHTS[p] * WEIGHTS[q] * WEIGHTS[r])
                block = jnp.concatenate(
                    [modulus_ref[p, 0, q, r], modulus_ref[p, 1, q, r]], axis=0
                )
                stiff_out[p * 25 + q * 5 + r] = weight * block
    for which, field in enumerate((prev_out, next_out, scale_out)):
        for k, v in enumerate(pack_low(sh, [field[qr] for qr in range(16)])):
            message[8 * which + k] = v


def count_kernel(receivers_ref, observed_ref, message, counts_out, far_out):
    contract = (((1,), (1,)), ((), ()))

    def counted(receivers, observed, nodes):
        row, lane = receiver_rows(receivers)
        row_hot = lax.broadcasted_iota(jnp.int32, (nodes, 128), 0) == row
        row_hot = jnp.where(row_hot, 1.0, 0.0).astype(BF16)
        lane_hot = lax.broadcasted_iota(jnp.int32, (128, 128), 0) == lane
        ones = jnp.where(lane_hot, 1.0, 0.0).astype(BF16)
        totals = [lax.dot_general(row_hot, ones, contract, preferred_element_type=F32)]
        for values in observed:
            total = None
            for part in split3(jnp.where(lane_hot, values, 0.0)):
                t = lax.dot_general(row_hot, part, contract, preferred_element_type=F32)
                total = t if total is None else total + t
            totals.append(total)
        return totals

    own = counted(receivers_ref[...], [observed_ref[0], observed_ref[1]], 512)
    for which, total in enumerate(own):
        for n in range(64):
            counts_out[which * 64 + n] = total[8 * n : 8 * n + 8]
    theirs = counted(
        message[16, 0:1, :].astype(jnp.int32), [message[16, 1:2, :], message[16, 2:3, :]], 128
    )
    for which, total in enumerate(theirs):
        for n in range(16):
            far_out[which * 16 + n] = half_turn(total[8 * n : 8 * n + 8])


def without_far(sh, field):
    def get(p, qr):
        if p < 4:
            return field[p * 16 + qr]
        return jnp.where(sh.low, half_turn(field[qr]), 0.0)

    return get


def force_kernel(u_ref, lam_ref, stiff, u_force, lam_force, blocks, scratch):
    sh = Shifts()
    for field, out in ((u_ref, u_force), (lam_ref, lam_force)):
        expand(sh, without_far(sh, field), blocks)
        force(sh, blocks, stiff, scratch, out)


def far_plane_kernel(
    slab_ref, message, stiff, u_in, lam_in, u_force, lam_force, far, near, column
):
    sh = Shifts()
    odd = is_odd(slab_ref)
    for n in range(25):
        f = backward_line([float(DERIVATIVE[k, 4]) * stiff[k * 25 + n] for k in range(5)])
        for k in range(5):
            column[k * 25 + n] = f[k]
    for which, (source, out) in enumerate(((u_in, u_force), (lam_in, lam_force))):
        face = [None] * 25
        for q in range(4):
            for r in range(4):
                v = jnp.where(sh.low, 0.0, to_high(message, 8 * which, q * 4 + r))
                face[q * 5 + r] = v
                if r == 0:
                    face[q * 5 + 4] = sh.next_z(v)
                if q == 0:
                    face[20 + r] = sh.next_y(v)
                    if r == 0:
                        face[24] = sh.next_z(face[20])
        for p in range(5):
            added = [column[p * 25 + n] * face[n] for n in range(25)]
            if p == 4:
                for a in range(5):
                    for at in ([a * 5 + k for k in range(5)], [k * 5 + a for k in range(5)]):
                        g = forward_line([face[n] for n in at])
                        f = backward_line([stiff[100 + n] * g[k] for k, n in enumerate(at)])
                        for k, n in enumerate(at):
                            added[n] = added[n] + f[k]
            for qr, v in enumerate(assemble(sh, added)):
                out[p * 16 + qr] = source[p * 16 + qr] + v
        put_messages(sh, odd, out, far, near, 8 * which)


def step_one_kernel(
    slab_ref,
    u_ref,
    lam_ref,
    prev_ref,
    next_ref,
    scale_ref,
    stiff,
    message0,
    message1,
    u_force,
    lam_force,
    far_in,
    near_in,
    u1_out,
    lam1_out,
    scale_out,
    u1_force,
    lam1_force,
    far,
    near,
    blocks,
    scratch,
):
    sh = Shifts()
    odd = is_odd(slab_ref)
    incoming = Incoming(odd, far_in, near_in)
    u0, lam2 = extended(sh, u_ref, message0, 0), extended(sh, lam_ref, message0, 8)
    before, after = extended(sh, prev_ref, message1, 0), extended(sh, next_ref, message1, 8)
    scale = extended(sh, scale_ref, message1, 16)
    u_total = assembled(sh, u_force, incoming, 0)
    lam_total = assembled(sh, lam_force, incoming, 8)
    for p in range(5):
        for qr in range(16):
            s = scale(p, qr)
            scale_out[p * 16 + qr] = s
            u1_out[p * 16 + qr] = 2.0 * u0(p, qr) - before(p, qr) - s * u_total(p, qr)
            lam1_out[p * 16 + qr] = 2.0 * lam2(p, qr) - after(p, qr) - s * lam_total(p, qr)
    for which, (field, out) in enumerate(((u1_out, u1_force), (lam1_out, lam1_force))):
        expand(sh, stored(field), blocks)
        force(sh, blocks, stiff, scratch, out)
        put_messages(sh, odd, out, far, near, 8 * which)


def mean_square(energy):
    total = jnp.sum(energy[3:4], axis=1, keepdims=True)
    return total / SAMPLES + EPSILON


def step_two_kernel(
    slab_ref,
    u_ref,
    lam_ref,
    message0,
    u1_ref,
    lam1_ref,
    scale,
    counts,
    far_counts,
    stiff,
    u1_force,
    lam1_force,
    far_in,
    near_in,
    u2_out,
    driven1_out,
    lam0_out,
    source_out,
    u3_out,
    driven1_force,
    far,
    near,
    blocks,
    scratch,
    u2_force,
):
    sh = Shifts()
    odd = is_odd(slab_ref)
    incoming = Incoming(odd, far_in, near_in)
    u0, lam2 = extended(sh, u_ref, message0, 0), extended(sh, lam_ref, message0, 8)

    def nodal(which):
        def get(p, qr):
            if p < 4:
                return counts[64 * which + p * 16 + qr]
            return jnp.where(
                sh.low, half_turn(counts[64 * which + qr]), far_counts[16 * which + qr]
            )

        return get

    count, seen = nodal(0), (nodal(1), nodal(2))
    u_total = assembled(sh, u1_force, incoming, 0)
    lam_total = assembled(sh, lam1_force, incoming, 8)
    for p in range(5):
        for qr in range(16):
            at = p * 16 + qr
            s, u1, c = scale[at], u1_ref[at], count(p, qr)
            u2 = 2.0 * u1 - u0(p, qr) - s * u_total(p, qr)
            u2_out[at] = u2
            driven1_out[at] = s * (c * u2 - seen[1](p, qr))
            source_out[at] = s * (c * u1 - seen[0](p, qr))
            lam0_out[at] = 2.0 * lam1_ref[at] - lam2(p, qr) - s * lam_total(p, qr)
    pairs = ((driven1_out, driven1_force), (u2_out, u2_force))
    for which, (field, out) in enumerate(pairs):
        expand(sh, stored(field), blocks)
        force(sh, blocks, stiff, scratch, out)
        put_messages(sh, odd, out, far, near, 8 * which)
    for at in range(64):
        f = u2_force[at]
        if at < 16:
            f = f + jnp.where(sh.low, 0.0, half_turn(u2_force[64 + at]))
        u3_out[at] = 2.0 * u2_out[at] - u1_ref[at] - scale[at] * f


def middle_kernel(
    u_ref,
    lam_ref,
    message0,
    u1_ref,
    lam1_ref,
    u2_ref,
    driven1_ref,
    lam0_ref,
    acc,
    driven_acc,
    first,
    second,
):
    sh = Shifts()
    expand(sh, stored(u1_ref), first)
    expand(sh, stored(driven1_ref), second)
    products(first, second, driven_acc, True)
    expand(sh, stored(lam1_ref), second)
    products(first, second, acc, True)
    expand(sh, stored(u2_ref), first)
    expand(sh, extended(sh, lam_ref, message0, 8), second)
    products(first, second, acc, False)
    expand(sh, extended(sh, u_ref, message0, 0), first)
    expand(sh, stored(lam0_ref), second)
    products(first, second, acc, False)


def last_kernel(
    slab_ref,
    event_ref,
    energy_ref,
    u_ref,
    message0,
    driven1_ref,
    scale,
    source,
    driven1_force,
    far_in,
    near_in,
    acc_ref,
    driven_acc_ref,
    out0,
    out1,
    out2,
    out3,
    driven0,
    first,
    second,
    acc,
    flat,
):
    sh = Shifts()
    total = assembled(sh, driven1_force, Incoming(is_odd(slab_ref), far_in, near_in), 0)
    for p in range(5):
        for qr in range(16):
            at = p * 16 + qr
            driven0[at] = 2.0 * driven1_ref[at] - scale[at] * total(p, qr) + source[at]
    expand(sh, extended(sh, u_ref, message0, 0), first)
    expand(sh, stored(driven0), second)
    for i in range(125):
        acc[i] = driven_acc_ref[i]
    products(first, second, acc, False)
    inverse = jnp.broadcast_to(1.0 / mean_square(energy_ref[...]), (8, 128))
    for p in range(5):
        for q in range(5):
            for r in range(5):
                at = p * 25 + q * 5 + r
                weight = float(-WEIGHTS[p] * WEIGHTS[q] * WEIGHTS[r])
                v = weight * (acc_ref[at] + inverse * acc[at])
                for i in range(2):
                    row = 4 * ((2 * p + i) * 25 + q * 5 + r)
                    flat[row : row + 4, :] = v[4 * i : 4 * i + 4]
    event = event_ref[0]
    for k, out in enumerate((out0, out1, out2, out3)):
        out[...] = flat[pl.ds(jnp.bitwise_xor(event, k), 250, stride=4), :]


def misfit_kernel(
    slab_ref,
    receivers_ref,
    observed_ref,
    u1_ref,
    u2_ref,
    u3_ref,
    scale,
    far_in,
    near_in,
    out,
    u3,
):
    sh = Shifts()
    incoming = Incoming(is_odd(slab_ref), far_in, near_in)
    for at in range(64):
        v = u3_ref[at]
        if at < 16:
            v = v - scale[at] * jnp.where(sh.low, incoming.from_left(8, at), 0.0)
        u3[at] = v
    row_hot, lane_hot = one_hots(receivers_ref[...])
    row_hot = jnp.where(row_hot, 1.0, 0.0).astype(BF16)
    squares = jnp.zeros((1, 128), F32)
    for step, field in enumerate((u1_ref, u2_ref, u3)):
        values = field[pl.ds(0, 64)].reshape(512, 128)
        picked = None
        for part in split3(values):
            t = lax.dot_general(
                part, row_hot, (((0,), (0,)), ((), ())), preferred_element_type=F32
            )
            picked = t if picked is None else picked + t
        syn = jnp.sum(jnp.where(lane_hot, picked, 0.0), axis=0, keepdims=True)
        residual = syn - observed_ref[step]
        squares = squares + residual * residual
    out[...] = jnp.broadcast_to(jnp.sum(squares, axis=1, keepdims=True), (1, 128))


def sum_kernel(a, b, c, d, misfit, total_out, message):
    total = a[...] + b[...] + c[...] + d[...]
    total_out[...] = total
    largest = jnp.max(jnp.max(jnp.abs(total), axis=0, keepdims=True), axis=1, keepdims=True)
    first_half = lax.broadcasted_iota(jnp.int32, (1, 128), 1) < 64
    message[...] = jnp.where(first_half, jnp.broadcast_to(largest, (1, 128)), misfit[...])


def divide_kernel(event_ref, total, gathered, energy_ref, out, misfit_out):
    rows = gathered[...]
    first_half = lax.broadcasted_iota(jnp.int32, (1, 128), 1) < 64
    top = jnp.where(first_half, jnp.max(rows, axis=0, keepdims=True), 0.0)
    largest = jnp.max(top, axis=1, keepdims=True)
    spaces = gathered.shape[0] // 4
    mine = gathered[pl.ds(pl.multiple_of(event_ref[0] * spaces, spaces), spaces), :]
    squares = jnp.where(first_half, 0.0, jnp.sum(mine, axis=0, keepdims=True))
    squares = jnp.max(squares, axis=1, keepdims=True)
    misfit_out[...] = jnp.broadcast_to(
        0.5 * squares / (SAMPLES * mean_square(energy_ref[...])), (1, 128)
    )
    out[...] = (total[...] / (largest + EPSILON)).reshape(250, 1, 128)


COST = 16 << 20
VMEM_GRANT = 8 << 20
VMEM_SPEC = pl.BlockSpec(memory_space=pltpu.VMEM)
SMEM_SPEC = pl.BlockSpec(memory_space=pltpu.SMEM)


def call(kernel, args, outs, scratch=(), scalars=0):
    return pl.pallas_call(
        kernel,
        out_shape=[jax.ShapeDtypeStruct(shape, F32) for shape in outs],
        in_specs=[SMEM_SPEC] * scalars + [VMEM_SPEC] * (len(args) - scalars),
        out_specs=[VMEM_SPEC] * len(outs),
        scratch_shapes=[pltpu.VMEM(shape, F32) for shape in scratch],
        cost_estimate=pl.CostEstimate(flops=0, bytes_accessed=COST, transcendentals=0),
        compiler_params=pltpu.CompilerParams(vmem_limit_bytes=VMEM_GRANT),
    )(*args)


def vectors(count):
    return (count, 8, 128)


def send(array, axis, pairs):
    return lax.ppermute(array, axis, pairs)


def to_left(array):
    devices = lax.axis_size("space")
    return send(array, "space", [(i, i - 1) for i in range(1, devices)])


def exchange(far, near):
    devices = lax.axis_size("space")
    far_pairs = [(i, i + 1 if i % 2 else i - 1) for i in range(1, devices - 1)]
    near_pairs = [(i, i - 1 if i % 2 else i + 1) for i in range(devices)]
    return (send(far, "space", far_pairs), send(near, "space", near_pairs))


def across(array, stride):
    devices = lax.axis_size("space")
    return array + send(array, "space", [(i, i ^ stride) for i in range(devices)])


def shards(state_now, state_prev, adjoint_now, adjoint_next, modulus, density, receivers, observed):
    slab = lax.axis_index("space").astype(jnp.int32).reshape(1)
    event = lax.axis_index("event").astype(jnp.int32).reshape(1)
    receivers = receivers.reshape(1, 128)
    observed = jnp.transpose(observed, (1, 0, 2))
    modulus = jnp.transpose(modulus, (0, 1, 2, 4, 3, 5))

    (facts,) = call(facts_kernel, (receivers, observed), [(4, 128)])
    energy = across(facts, 1)

    u0, lam2, planes = call(
        first_kernel,
        (jnp.stack([state_now[0], adjoint_now[0]]), facts),
        [vectors(64), vectors(64), vectors(17)],
        [(4, 128, 128)],
    )
    message0 = to_left(planes)
    energy = across(energy, 16)
    before, after, scale, stiff, planes = call(
        second_kernel,
        (slab, jnp.stack([state_prev[0], adjoint_next[0], density]), modulus),
        [vectors(64), vectors(64), vectors(64), vectors(125), vectors(24)],
        [(4, 128, 128)],
        scalars=1,
    )
    u_force, lam_force = call(
        force_kernel,
        (u0, lam2, stiff),
        [vectors(80), vectors(80)],
        [vectors(125), vectors(125)],
    )
    message1 = to_left(planes)
    energy = across(energy, 2)
    counts, far_counts = call(
        count_kernel, (receivers, observed, message0), [vectors(192), vectors(48)]
    )
    u_force, lam_force, far, near = call(
        far_plane_kernel,
        (slab, message0, stiff, u_force, lam_force),
        [vectors(80), vectors(80), vectors(16), vectors(16)],
        [vectors(125)],
        scalars=1,
    )
    energy = across(energy, 32)
    far, near = exchange(far, near)
    u1, lam1, scale, u1_force, lam1_force, far, near = call(
        step_one_kernel,
        (
            slab,
            u0,
            lam2,
            before,
            after,
            scale,
            stiff,
            message0,
            message1,
            u_force,
            lam_force,
            far,
            near,
        ),
        [vectors(80)] * 5 + [vectors(16)] * 2,
        [vectors(125), vectors(125)],
        scalars=1,
    )
    energy = across(energy, 4)
    energy = across(energy, 8)
    far, near = exchange(far, near)
    u2, driven1, lam0, source, u3, driven1_force, far, near = call(
        step_two_kernel,
        (
            slab,
            u0,
            lam2,
            message0,
            u1,
            lam1,
            scale,
            counts,
            far_counts,
            stiff,
            u1_force,
            lam1_force,
            far,
            near,
        ),
        [vectors(80)] * 4 + [vectors(64), vectors(80)] + [vectors(16)] * 2,
        [vectors(125), vectors(125), vectors(80)],
        scalars=1,
    )
    far, near = exchange(far, near)
    acc, driven_acc = call(
        middle_kernel,
        (u0, lam2, message0, u1, lam1, u2, driven1, lam0),
        [vectors(125), vectors(125)],
        [vectors(125), vectors(125)],
    )
    pieces = call(
        last_kernel,
        (
            slab,
            event,
            energy,
            u0,
            message0,
            driven1,
            scale,
            source,
            driven1_force,
            far,
            near,
            acc,
            driven_acc,
        ),
        [(250, 128)] * 4,
        [vectors(80), vectors(125), vectors(125), vectors(125), (1000, 128)],
        scalars=2,
    )
    events = lax.axis_size("event")
    others = [send(pieces[k], "event", [(i, i ^ k) for i in range(events)]) for k in (1, 2, 3)]
    (squares,) = call(
        misfit_kernel,
        (slab, receivers, observed, u1, u2, u3, scale, far, near),
        [(1, 128)],
        [vectors(64)],
        scalars=1,
    )
    total, message = call(
        sum_kernel, (pieces[0], *others, squares), [(250, 128), (1, 128)]
    )
    everyone = ("event", "space")
    devices = lax.axis_size("event") * lax.axis_size("space")
    gathered = lax.all_to_all(
        jnp.broadcast_to(message[None], (devices, 1, 128)), everyone, 0, 0
    )
    kernel, misfit = call(
        divide_kernel,
        (event, total, gathered.reshape(devices, 128), energy),
        [(250, 1, 128), (1, 128)],
        scalars=1,
    )
    kernel = jnp.transpose(kernel.reshape(5, 2, 5, 5, 1, 128), (0, 1, 2, 4, 3, 5))
    return (kernel, misfit[0, :1])


def solution(mesh):
    in_specs = (
        P("event", "space", None, None),
        P("event", "space", None, None),
        P("event", "space", None, None),
        P("event", "space", None, None),
        P(None, "space", None, None, None, None),
        P("space", None, None),
        P("space"),
        P("event", None, "space"),
    )
    out_specs = (P(None, "space", None, "event", None, None), P("event"))

    return jax.shard_map(shards, mesh=mesh, in_specs=in_specs, out_specs=out_specs, check_vma=False)
```
